128 devices in a mesh: rows: 32 (over z, y, core), aux: 4 (over x).
Axes of the slice: x: 4, y: 4, z: 4, core: 2. Of those that a mesh axis runs over, the one named last changes fastest.
Arguments:
- density: bfloat16 [128, 8, 16384], P('aux', None, 'rows'), may hold values from -64 to 64, as said below
- vir_coeffs: bfloat16 [16384, 16384], P('rows'), may hold values from -0.046875 to 0.046875
- occ_coeffs: bfloat16 [8, 16384], P(None, 'rows'), may hold values from -2 to 2
- shell_len: int32 [32, 64], replicated, may hold values from 1 to 16, 512 in all within a row
- mu_shell: int32 [8192], P('rows'), may hold values from 0 to 2047
- nu_shell: int32 [8192], P('rows'), may hold values from 0 to 63
- owner: int32 [8192, 1], P('rows'), may hold values from 0 to 31; in each aligned block of 256 rows (0 to 255, 256 to 511, ...) at most 16 rows name the same one
Outputs:
- pair_blocks: bfloat16 [16384, 128, 256], P('rows', 'aux')
- pair_scale: float32 [16384], P('rows')
The draws below stay inside these ranges and needn't reach their ends.
Inputs may be any that keep to these rules, and one draw needn't show every extreme that they name: Each index of rows names at most 16 of its 256 pairs for one owner, and exactly 16 for some owner. `shell_len`: shell lengths of each slab sum to 512; the longest is 16. `density`: Real-valued, of varying scale over auxiliary functions and orbital pairs.
All inputs are finite; a program needn't handle non-finite values.
Results may differ from the reference program's by a relative error of at most 0.0049.
Values may be sent and summed in bfloat16 or wider, within the bound.
A program may use at most 192 MiB of HBM per device.

```python
import math
import jax
import jax.numpy as jnp
import numpy as np
from jax import lax

O = 8
NAUX = 128
NAO_DEV = 512
SH_DEV = 64
PAD = 16
PAIRS_DEV = 256
V = 16384
NAO = 16384
NSH = 2048
CAP = 16
NPAIR = 8192
SLOTS = 16384
N_ROWS = 32


def draw_density(key, part):
    key_base, key_row, key_col = jax.random.split(jax.random.fold_in(key, 17), 3)
    ramp = 3.0 ** (jnp.arange(NAUX, dtype=jnp.float32) / (NAUX - 1))
    row_scale = ramp * jnp.exp(jax.random.uniform(key_row, (NAUX,), minval=0.0, maxval=math.log(3.5)))
    col_scale = jnp.exp(jax.random.uniform(key_col, (O, V), minval=0.0, maxval=math.log(10.0)))
    base = jnp.clip(jax.random.normal(key_base, (NAUX, O, V), dtype=jnp.float32), -6.0, 6.0)
    values = 0.1 * base * row_scale[:, None, None] * col_scale[None, :, :]
    return values.astype(jnp.bfloat16)


def place_ends(array, key, least, largest):
    extent = array.shape
    spot = [jax.random.randint(jax.random.fold_in(key, axis), (), 0, extent[axis]) for axis in range(len(extent))]
    array = array.at[tuple(spot)].set(least)
    longest = extent.index(max(extent))
    spot[longest] = (spot[longest] + 1) % extent[longest]
    return array.at[tuple(spot)].set(largest)


def shard_levels(stream_key, shape, cuts, low, high):
    def one(axis_at, parts):
        draws = jax.random.uniform(jax.random.fold_in(jax.random.fold_in(stream_key, 6), axis_at), (parts,), jnp.float32, low / len(cuts), high / len(cuts))
        return jnp.repeat(jnp.exp(draws), shape[axis_at] // parts).reshape((-1,) + (1,) * (len(shape) - axis_at - 1))

    level = one(*cuts[0])
    for cut in cuts[1:]:
        level = level * one(*cut)
    return level


def split_up(amount, total, reach, lean):
    loads = [(1 << 20) // math.isqrt(grade ** lean) + 1 for grade in range(2, amount + 1)]
    spare, counts = total - reach - (amount - 1), [1] * (amount - 1)
    while spare > 0:
        free = [i for i in range(amount - 1) if counts[i] < reach]
        whole, remaining = sum([loads[i] for i in free]), spare
        for i in free:
            more = min(reach - counts[i], max(1, remaining * loads[i] // whole), spare)
            counts[i] = counts[i] + more
            spare = spare - more
    return np.array([reach] + counts)


def ragged_sizes(key, count, total, most, skew):
    if count == 2:
        one = jax.random.randint(key, (), max(1, total - most), min(most, total - 1) + 1)
        return jnp.stack([one, total - one])
    sizes = jnp.asarray(split_up(count, total, most, skew), jnp.int32)
    pairs = (count - 1) // 2
    giver, sink = sizes[1:1 + 2 * pairs:2], sizes[2:2 + 2 * pairs:2]
    slack = jnp.minimum(giver - 1, most - sink)
    passed = jax.random.randint(jax.random.fold_in(key, 1), (pairs,), 0, 1 << 20) % (slack + 1)
    sizes = sizes.at[1:1 + 2 * pairs:2].set(giver - passed).at[2:2 + 2 * pairs:2].set(sink + passed)
    return sizes[jax.random.permutation(jax.random.fold_in(key, 2), count)]


def assign_block(stream_key, own, number, rows, count, top, limit, lean):
    sequence = jax.random.permutation(stream_key, count)
    crowded, usual = load_shares(count, rows * top, limit, lean, True), load_shares(count, rows * top, limit, lean, False)
    places = jnp.arange(count)

    def named(lengths, turn):
        used = int((lengths > 0).sum())
        fixed = max(1, used // 4)
        moved = fixed + (places - fixed + turn * (used - fixed)) % max(1, count - fixed)
        return jnp.zeros((count,), jnp.int32).at[sequence[jnp.where(places < fixed, places, moved)]].set(jnp.asarray(lengths, jnp.int32))

    lengths = jnp.where(number % 4 == 0, named(crowded, number // 4), named(usual, number - number // 4 - 1))
    mixed = jax.random.permutation(jax.random.fold_in(own, 3), count)
    giver, sink = mixed[0:count // 2 * 2:2], mixed[1:count // 2 * 2:2]
    margin = jnp.minimum(lengths[giver] - 1, limit - lengths[sink]) // 2
    margin = jnp.where((giver == sequence[0]) | (sink == sequence[0]) | (lengths[sink] == 0), 0, jnp.maximum(margin, 0))
    moved = jax.random.randint(jax.random.fold_in(own, 4), (count // 2,), 0, 1 << 20) % (margin + 1)
    lengths = lengths.at[giver].add(-moved).at[sink].add(moved)
    members = jnp.searchsorted(jnp.cumsum(lengths), jnp.arange(rows * top), side="right").astype(jnp.int32)
    listing = members.reshape(top, rows).T
    listing = listing[jax.random.permutation(jax.random.fold_in(own, 1), rows)]
    turn = jax.random.randint(jax.random.fold_in(own, 2), (rows, 1), 0, top)
    return jnp.take_along_axis(listing, (jnp.arange(top)[None, :] + turn) % top, axis=1)


def load_shares(count, total, most, slope, full):
    loads = [(1 << 20) // math.isqrt(standing ** slope) + 1 for standing in range(1, count + 1)]
    largest = most if full else min(most, max(-(-total // count), total * loads[0] // sum(loads)))
    least = 1 if total - largest >= count - 1 else 0
    holding, surplus = [largest] + [least] * (count - 1), total - largest - least * (count - 1)
    while surplus > 0:
        movable = [i for i in range(1, count) if holding[i] < largest] or [i for i in range(1, count) if holding[i] < most]
        pool, left = sum([loads[i] for i in movable]), surplus
        for i in movable:
            extra = min(most - holding[i], max(1, left * loads[i] // pool), surplus)
            holding[i] = holding[i] + extra
            surplus = surplus - extra
    return np.array(holding)


def gaussian(own_key, dims, spread, limit, cuts=(), kind=jnp.bfloat16):
    values = jax.random.normal(own_key, dims, jnp.float32) * spread
    if len(cuts) > 0:
        values = shard_levels(own_key, dims, cuts, -0.22, 0.18) * values
    return jnp.clip(values, min=-limit, max=limit).astype(kind)


def setup_inputs(seed: int = 0) -> dict:
    key_of = jax.random.split(jax.random.key(seed), 8)
    density = draw_density(jax.random.fold_in(key_of[7], 71), 0)
    vir_coeffs = gaussian(key_of[1], (NAO, V), V ** -0.5, 0.046875, ((0, 32),))
    occ_coeffs = gaussian(key_of[2], (O, NAO), O ** -0.5, 2.0, ((1, 32),))
    shell_len = jax.vmap(lambda own: ragged_sizes(own, SH_DEV, NAO_DEV, PAD, 2))(jax.random.split(key_of[3], N_ROWS)).reshape((N_ROWS, SH_DEV)).astype(jnp.int32)
    mu_shell = place_ends(jax.random.randint(key_of[4], (NPAIR,), 0, NSH), jax.random.fold_in(key_of[4], 1), 0, NSH - 1).astype(jnp.int32)
    nu_shell = place_ends(jax.random.randint(key_of[5], (NPAIR,), 0, SH_DEV), jax.random.fold_in(key_of[5], 1), 0, SH_DEV - 1).astype(jnp.int32)
    owner_keys = jax.random.split(jax.random.fold_in(key_of[6], 1), NPAIR // PAIRS_DEV)
    owner_turns = jax.random.permutation(jax.random.fold_in(key_of[6], 3), NPAIR // PAIRS_DEV)
    owner = jax.vmap(lambda own, number: assign_block(jax.random.fold_in(key_of[6], 2), own, number, PAIRS_DEV, N_ROWS, 1, CAP, 2))(owner_keys, owner_turns).reshape((NPAIR, 1))
    return dict(density=density, vir_coeffs=vir_coeffs, occ_coeffs=occ_coeffs, shell_len=shell_len, mu_shell=mu_shell, nu_shell=nu_shell, owner=owner)


def lookup(table, index):
    hits = index[:, None] == jnp.arange(table.shape[0], dtype=jnp.int32)[None, :]
    return lax.optimization_barrier(jnp.sum(jnp.where(hits, table[None, :], 0), axis=1)).astype(jnp.int32)

def reference(density, vir_coeffs, occ_coeffs, shell_len, mu_shell, nu_shell, owner):
    flat = density.reshape(NAUX * O, V)
    half = jnp.dot(flat, vir_coeffs.T, preferred_element_type=jnp.float32).astype(jnp.bfloat16).reshape(NAUX, O, NAO)
    starts = jnp.cumsum(shell_len, axis=1) - shell_len
    flat_start = (starts + jnp.arange(N_ROWS, dtype=jnp.int32)[:, None] * NAO_DEV).reshape(-1).astype(jnp.int32)
    flat_len = shell_len.reshape(-1).astype(jnp.int32)
    source = jnp.arange(NPAIR, dtype=jnp.int32) // PAIRS_DEV
    mu_start = lookup(flat_start, mu_shell)
    mu_len = lookup(flat_len, mu_shell)
    nu_global = (source * SH_DEV + nu_shell).astype(jnp.int32)
    nu_start = lookup(flat_start, nu_global)
    nu_len = lookup(flat_len, nu_global)
    dest = owner[:, 0]
    onehot = (dest[:, None] == jnp.arange(N_ROWS, dtype=jnp.int32)[None, :]).astype(jnp.int32)
    onehot = onehot.reshape(N_ROWS, PAIRS_DEV, N_ROWS)
    earlier = jnp.cumsum(onehot, axis=1) - onehot
    rank = lax.optimization_barrier(jnp.sum(earlier * onehot, axis=2)).reshape(-1)
    slot = (dest * (N_ROWS * CAP) + source * CAP + rank).astype(jnp.int32)
    half_pad = jnp.pad(half, ((0, 0), (0, 0), (0, PAD)))
    occ_pad = jnp.pad(occ_coeffs, ((0, 0), (0, PAD)))
    offsets = jnp.arange(PAD, dtype=jnp.int32)

    def one_source(packed):
        mu_first, mu_count, nu_first, nu_count = packed
        h_tiles = jax.vmap(lambda start: lax.dynamic_slice_in_dim(half_pad, start, PAD, 2))(nu_first)
        h_tiles = jnp.where((offsets[None, :] < nu_count[:, None])[:, None, None, :], h_tiles, 0)
        c_tiles = jax.vmap(lambda start: lax.dynamic_slice_in_dim(occ_pad, start, PAD, 1))(mu_first)
        c_tiles = jnp.where((offsets[None, :] < mu_count[:, None])[:, None, :], c_tiles, 0)
        blocks = jnp.einsum('kim,kpin->kpmn', c_tiles.astype(jnp.float32), h_tiles.astype(jnp.float32))
        blocks = blocks.astype(jnp.bfloat16).reshape(PAIRS_DEV, NAUX, PAD * PAD)
        squares = lax.optimization_barrier(jnp.sum(jnp.square(blocks.astype(jnp.float32)), axis=(1, 2)))
        return (blocks, squares)
    packed = (mu_start.reshape(N_ROWS, PAIRS_DEV), mu_len.reshape(N_ROWS, PAIRS_DEV), nu_start.reshape(N_ROWS, PAIRS_DEV), nu_len.reshape(N_ROWS, PAIRS_DEV))
    blocks, squares = lax.map(one_source, packed)
    blocks = blocks.reshape(NPAIR, NAUX, PAD * PAD)
    squares = squares.reshape(NPAIR)
    pair_blocks = jnp.zeros((SLOTS, NAUX, PAD * PAD), jnp.bfloat16).at[slot].set(blocks)
    total = jnp.zeros((SLOTS,), jnp.float32).at[slot].set(squares)
    pair_scale = jnp.sqrt(total / (NAUX * PAD * PAD) + 1e-06)
    return (pair_blocks, pair_scale)
```

```python
import jax
import jax.numpy as jnp
from jax import lax
from jax.experimental import pallas as pl
from jax.experimental.pallas import tpu as pltpu
from jax.sharding import PartitionSpec as P

NY = 4
NZ = 4
NCHIP = NY * NZ
NROW = 2 * NCHIP
NX = 4
UNITS = 4
OCC = 8
PAD = 16
CAP = 16
F32 = jnp.float32
BF16 = jnp.bfloat16
I32 = jnp.int32
ORDER = [(0, 0), (1, 0), (0, 1), (3, 0), (0, 3), (2, 0), (0, 2), (1, 1), (3, 3), (1, 3), (3, 1),
         (2, 1), (1, 2), (2, 3), (3, 2), (2, 2)]


def pick(t, values):
    out = jnp.int32(values[0])
    for k in range(1, len(values)):
        out = jnp.where(t == k, jnp.int32(values[k]), out)
    return out


def iota(shape, dim):
    return lax.broadcasted_iota(I32, shape, dim)


def dot(a, b):
    return lax.dot_general(a, b, (((1,), (0,)), ((), ())), preferred_element_type=F32)


def dot_nt(a, b):
    return lax.dot_general(a, b, (((1,), (1,)), ((), ())), preferred_element_type=F32)


def kernel(dens, vir, extra, slen, out, total_out,
           dg, hg, cbuf, eg, acc, occf, spread, rolled, cexp, squares, sumbuf, sumout, vtab,
           stab, ptab,
           dens_sem, vir_sem, d_recv, h_recv, d_send, h_send, e_send, x_recv, x_send, t_sem):
    row = lax.axis_index("rows")
    ax = lax.axis_index("aux")
    core = lax.rem(row, 2)
    y = lax.rem(row // 2, NY)
    z = row // (2 * NY)

    def rid(zz, yy, cc):
        return (lax.rem(zz, NZ) * NY + lax.rem(yy, NY)) * 2 + cc

    sib = rid(z, y, 1 - core)
    peers = {
        ("y", 1): rid(z, y + 1, core),
        ("y", -1): rid(z, y + NY - 1, core),
        ("z", 1): rid(z + 1, y, core),
        ("z", -1): rid(z + NZ - 1, y, core),
    }
    own_d = pltpu.make_async_copy(dens, dg.at[row], dens_sem.at[0])
    own_e = pltpu.make_async_copy(extra, eg.at[row], dens_sem.at[1])
    own_d.start()
    own_e.start()

    def chip_of(t):
        dy, dz = pick(t, [o[0] for o in ORDER]), pick(t, [o[1] for o in ORDER])
        return lax.rem(z + dz, NZ) * NY + lax.rem(y + dy, NY), dy, dz

    def vir_copy(t):
        q, _, _ = chip_of(t)
        return pltpu.make_async_copy(
            vir.at[:, pl.ds(pl.multiple_of(q * 1024, 1024), 1024)], cbuf.at[q], vir_sem.at[t])

    def start_vir(t, _):
        vir_copy(t).start()
        return 0

    barrier = pltpu.get_barrier_semaphore()
    targets = [(p, ax) for p in peers.values()] + [(sib, ax)]
    targets += [(row, lax.rem(ax + k, NX)) for k in range(1, NX)]
    for target in targets:
        pl.semaphore_signal(barrier, inc=1, device_id=target, device_id_type=pl.DeviceIdType.MESH)
    pl.semaphore_wait(barrier, len(targets))
    own_d.wait()
    own_e.wait()

    def gather(units, recv, compute, before):
        def send(k, r, target):
            ref_of, sem, _, _ = units[k]
            pltpu.make_async_remote_copy(
                ref_of(r), ref_of(r), sem, recv.at[k, r],
                device_id=(target, ax), device_id_type=pl.DeviceIdType.MESH).start()

        def wait(k, r):
            ref_of, sem, _, _ = units[k]
            pltpu.make_async_remote_copy(
                ref_of(r), ref_of(r), sem, recv.at[k, r],
                device_id=(sib, ax), device_id_type=pl.DeviceIdType.MESH).wait_recv()

        other = {"y": "z", "z": "y"}
        n = len(units)
        for phase in range(2):
            for k in range(n):
                axis = units[k][2] if phase == 0 else other[units[k][2]]
                send(k, row, peers[(axis, 1)])
                send(k, row, peers[(axis, -1)])
        for k in range(n):
            send(k, row, sib)
        before()

        def step(t, _):
            @pl.when(t < NCHIP)
            def _():
                q, dy, dz = chip_of(t)
                r = q * 2 + core
                for k in range(n):
                    _, _, axis, sgn = units[k]
                    du, dv = (dy, dz) if axis == "y" else (dz, dy)
                    back = NY - 1 if sgn == 1 else 1
                    wait(k, r)

                    @pl.when((du == back) & (dv == 0))
                    def _():
                        send(k, r, peers[(axis, sgn)])

                    @pl.when(dv == 0)
                    def _():
                        send(k, r, peers[(other[axis], 1)])
                        send(k, r, peers[(other[axis], -1)])

                    @pl.when(dv == back)
                    def _():
                        send(k, r, peers[(other[axis], sgn)])

                for k in range(n):
                    send(k, r, sib)

            q, _, _ = chip_of(t - 1)
            for k in range(n):
                wait(k, q * 2 + 1 - core)
            compute(t - 1, q)
            return 0

        lax.fori_loop(1, NCHIP + 1, step, 0)

    def rows_of(buf, k):
        return lambda r: buf.at[r, pl.ds(64 * k, 64)]

    shape_of = [("y", 1), ("z", 1), ("y", -1), ("z", -1)]
    d_units = [(rows_of(dg, k), d_send.at[k]) + shape_of[k] for k in range(UNITS)]
    d_units.append((lambda r: eg.at[r], e_send.at[0], "y", 1))
    h_units = [(rows_of(hg, k), h_send.at[k]) + shape_of[k] for k in range(UNITS)]

    def before_d():
        lax.fori_loop(0, NCHIP, start_vir, 0)
        acc[...] = jnp.zeros_like(acc)
        spread[...] = (iota((128, 256), 0) == iota((128, 256), 1) // PAD).astype(F32).astype(BF16)

    def compute_d(t, q):
        vir_copy(t).wait()
        part = dot_nt(dg[2 * q], cbuf[q, :, 0:512]) + dot_nt(dg[2 * q + 1], cbuf[q, :, 512:1024])
        for b in range(4):
            acc[b] += part[:, 128 * b:128 * b + 128]

    gather(d_units, d_recv, compute_d, before_d)

    for i in range(OCC):
        for b in range(4):
            hg[row, 32 * i:32 * i + 32, 128 * b:128 * b + 128] = acc[b, pl.ds(i, 32, stride=OCC), :].astype(BF16)

    def before_h():
        lens = slen[...]
        lens_f = lens.astype(F32)
        lower = (iota((64, 64), 0) < iota((64, 64), 1)).astype(F32).astype(BF16)
        starts = dot(lens_f.astype(BF16), lower)
        vtab[0, :, 0:64] = (starts * 32.0 + lens_f).astype(I32)
        meta = eg[:, 8:10, :].astype(F32)
        own = meta[:, 0, 0:256]
        nu = meta[:, 0, 256:512]
        code = meta[:, 1, 0:256] * 4096.0 + meta[:, 1, 256:512] * 64.0 + nu + 131072.0
        match = own == row.astype(F32)
        match_f = match.astype(F32)
        upper = (iota((256, 256), 0) < iota((256, 256), 1)).astype(F32).astype(BF16)
        rank = dot(match_f.astype(BF16), upper)
        lane = iota((NROW, 128), 1)
        table = jnp.zeros((NROW, 128), F32)
        for r in range(CAP):
            val = jnp.sum(jnp.where(match & (rank == float(r)), code, 0.0), axis=1, keepdims=True)
            table = jnp.where(lane == r, val, table)
        vtab[1] = table.astype(I32)
        c0 = pltpu.make_async_copy(vtab.at[0], stab, t_sem.at[0])
        c1 = pltpu.make_async_copy(vtab.at[1], ptab, t_sem.at[1])
        c0.start()
        c1.start()
        for r in range(NROW):
            piece = eg[r, 0:8, :].astype(F32)
            for b in range(4):
                occf[4 * r + b] = piece[:, 128 * b:128 * b + 128]
        c0.wait()
        c1.wait()

    lane8 = iota((8, 128), 1)
    lane256 = iota((1, 256), 1)

    def blocks(j):
        target = jnp.full((1, 256), -1, I32)
        for r in range(CAP):
            v = ptab[j, r]
            live = (v >> 17) & 1
            nu_w = stab[j, v & 63]
            rho = (v >> 12) & 31
            mu_w = stab[rho, (v >> 6) & 63]
            q0 = (mu_w >> 5) & 511
            mu_len = (mu_w & 31) * live
            n0 = (nu_w >> 5) & 511
            nu_len = (nu_w & 31) * live
            b = q0 >> 7
            off = q0 & 127
            left = occf[rho * 4 + b]
            right = occf[rho * 4 + jnp.minimum(b + 1, 3)]
            shift = (128 - off) & 127
            tile = jnp.where(lane8 < 128 - off, pltpu.roll(left, shift, 1), pltpu.roll(right, shift, 1))
            rolled[8 * r:8 * r + 8, :] = jnp.where(lane8 < mu_len, tile, 0.0)
            inner = lane256 - r * PAD
            target = jnp.where((inner >= 0) & (inner < nu_len), inner + n0, target)
        cexp[...] = dot(rolled[...].astype(BF16), spread[...])
        select = (iota((512, 256), 0) == target).astype(F32).astype(BF16)
        tiles = dot(hg[j], select)
        lane = iota((32, 128), 1)
        mask_n = (iota((PAD, 256), 0) == iota((PAD, 256), 1) % PAD).astype(F32)
        for g in range(2):
            xs = [tiles[32 * i:32 * i + 32, 128 * g:128 * g + 128] for i in range(OCC)]
            for bit in (1, 2, 4):
                low = (lane // (PAD * bit)) % 2 == 0
                ys = list(xs)
                for i in range(OCC):
                    if i & bit:
                        continue
                    a, c = xs[i], xs[i | bit]
                    ys[i] = jnp.where(low, a, pltpu.roll(c, PAD * bit, 1))
                    ys[i | bit] = jnp.where(low, pltpu.roll(a, 128 - PAD * bit, 1), c)
                xs = ys
            for s in range(8):
                slot = 8 * g + s
                coeff = jnp.concatenate(
                    [(cexp[8 * slot + i:8 * slot + i + 1, :] * mask_n).astype(BF16) for i in range(OCC)], axis=0)
                block = dot(xs[s].astype(BF16), coeff).astype(BF16)
                out[j * CAP + slot] = block
                wide = block.astype(F32)
                sq = wide * wide
                sq = sq[:, 0:128] + sq[:, 128:256]
                squares[j, slot:slot + 1, :] = jnp.sum(sq, axis=0, keepdims=True)

    def compute_h(t, q):
        def one(c, _):
            blocks(2 * q + c)
            return 0

        lax.fori_loop(0, 2, one, 0)

    gather(h_units, h_recv, compute_h, before_h)

    diag = iota((128, 128), 0) == iota((128, 128), 1)
    for b in range(4):
        part = squares[8 * b:8 * b + 8].reshape(128, 128)
        lanes = jnp.sum(part, axis=1, keepdims=True)
        sumout[b:b + 1, :] = jnp.sum(jnp.where(diag, lanes, 0.0), axis=0, keepdims=True)
    sumout[4:8, :] = jnp.zeros((4, 128), F32)
    sumbuf[ax] = sumout[...]
    copies = []
    for k in range(1, NX):
        peer = lax.rem(ax + k, NX)
        copy = pltpu.make_async_remote_copy(
            sumout, sumbuf.at[ax], x_send.at[k], x_recv.at[k],
            device_id=(row, peer), device_id_type=pl.DeviceIdType.MESH)
        copy.start()
        copies.append(copy)
    for copy in copies:
        copy.wait_recv()
    total_out[...] = (sumbuf[0] + sumbuf[1]) + (sumbuf[2] + sumbuf[3])
    for copy in copies:
        copy.wait_send()
    for k in range(UNITS):
        for buf, sem in ((dg, d_send), (hg, h_send)):
            ref = buf.at[pl.ds(0, 31), pl.ds(64 * k, 64)]
            pltpu.make_async_copy(ref, ref, sem.at[k]).wait()
    ref = eg.at[pl.ds(0, 31)]
    pltpu.make_async_copy(ref, ref, e_send.at[0]).wait()


def per_device(density, vir_coeffs, occ_coeffs, shell_len, mu_shell, nu_shell, owner):
    dens = density.reshape(256, 512)
    meta = jnp.concatenate([owner[:, 0], nu_shell, mu_shell // 64, mu_shell % 64]).reshape(2, 512).astype(BF16)
    extra = jnp.concatenate([occ_coeffs, meta, jnp.zeros((6, 512), BF16)], axis=0)
    vmem = pl.BlockSpec(memory_space=pltpu.VMEM)
    hbm = pl.BlockSpec(memory_space=pl.ANY)
    blocks, total = pl.pallas_call(
        kernel,
        out_shape=(pltpu.VMEM((512, 32, 256), BF16), jax.ShapeDtypeStruct((8, 128), F32)),
        in_specs=[hbm, hbm, hbm, vmem],
        out_specs=(pl.BlockSpec(memory_space=pltpu.VMEM), vmem),
        scratch_shapes=[
            pltpu.VMEM((NROW, 256, 512), BF16),
            pltpu.VMEM((NROW, 256, 512), BF16),
            pltpu.VMEM((NCHIP, 512, 1024), BF16),
            pltpu.VMEM((NROW, 16, 512), BF16),
            pltpu.VMEM((4, 256, 128), F32),
            pltpu.VMEM((4 * NROW, 8, 128), F32),
            pltpu.VMEM((128, 256), BF16),
            pltpu.VMEM((128, 128), F32),
            pltpu.VMEM((128, 256), F32),
            pltpu.VMEM((NROW, CAP, 128), F32),
            pltpu.VMEM((NX, 8, 128), F32),
            pltpu.VMEM((8, 128), F32),
            pltpu.VMEM((2, NROW, 128), I32),
            pltpu.SMEM((NROW, 128), I32),
            pltpu.SMEM((NROW, 128), I32),
            pltpu.SemaphoreType.DMA((2,)),
            pltpu.SemaphoreType.DMA((NCHIP,)),
            pltpu.SemaphoreType.DMA((UNITS + 1, NROW)),
            pltpu.SemaphoreType.DMA((UNITS, NROW)),
            pltpu.SemaphoreType.DMA((UNITS,)),
            pltpu.SemaphoreType.DMA((UNITS,)),
            pltpu.SemaphoreType.DMA((1,)),
            pltpu.SemaphoreType.DMA((NX,)),
            pltpu.SemaphoreType.DMA((NX,)),
            pltpu.SemaphoreType.DMA((2,)),
        ],
        compiler_params=pltpu.CompilerParams(
            collective_id=0, has_side_effects=True, vmem_limit_bytes=48 * 1024 * 1024),
    )(dens, vir_coeffs, extra, shell_len)
    pair_scale = jnp.sqrt(total[0:4].reshape(512) / (128 * PAD * PAD) + 1e-06)
    return blocks, pair_scale


def solution(mesh):
    return jax.shard_map(
        per_device,
        mesh=mesh,
        in_specs=(
            P("aux", None, "rows"),
            P("rows", None),
            P(None, "rows"),
            P(),
            P("rows"),
            P("rows"),
            P("rows", None),
        ),
        out_specs=(P("rows", "aux", None), P("rows")),
        check_vma=False,
    )
```

```python
import jax
import jax.numpy as jnp
from jax import lax
from jax.experimental import pallas as pl
from jax.experimental.pallas import tpu as pltpu
from jax.sharding import PartitionSpec as P

NY = 4
NZ = 4
NCHIP = NY * NZ
NROW = 2 * NCHIP
NX = 4
UNITS = 4
OCC = 8
PAD = 16
CAP = 16
F32 = jnp.float32
BF16 = jnp.bfloat16
I32 = jnp.int32
ROUNDS = [(3, 0), (1, 0), (0, 3), (0, 1), (2, 0), (3, 3), (3, 1), (1, 3), (1, 1), (0, 2), (2, 3), (2, 1), (3, 2), (1, 2), (2, 2)]
COMPUTE = [(0, 0), (1, 0), (3, 0), (0, 1), (0, 3), (3, 3), (1, 1), (3, 1), (1, 3), (2, 0), (0, 2), (3, 2), (2, 3), (1, 2), (2, 1), (2, 2)]
COUNTS = [1, 0, 0, 2, 1, 1, 1, 0, 1, 1, 1, 2, 2, 2, 1]


def iota(shape, dim):
    return lax.broadcasted_iota(I32, shape, dim)


def dot(a, b):
    return lax.dot_general(a, b, (((1,), (0,)), ((), ())), preferred_element_type=F32)


def dot_nt(a, b):
    return lax.dot_general(a, b, (((1,), (1,)), ((), ())), preferred_element_type=F32)


def packed(values, bits=2):
    word = 0
    for k, v in enumerate(values):
        word |= (v % (1 << bits)) << (bits * k)
    return jnp.int32(word - (1 << 32) if word >= 1 << 31 else word)


def entry(word, t, bits=2):
    return lax.shift_right_logical(word, bits * t) & ((1 << bits) - 1)


def kernel(dens, vir, occ, slen_h, mu_h, nu_h, own_h, out, total_out,
           dg, hg, cbuf, eo, em, slen, acc, occf, spread, repeat, rolled, cexp, targets, squares, sumbuf, sumout, vtab, wtab,
           stab, ptab,
           in_sem, vir_sem, d_recv, h_recv, o_recv, m_recv, d_send, h_send, o_send, m_send, x_recv, x_send, t_sem):
    row = lax.axis_index("rows")
    ax = lax.axis_index("aux")
    core = lax.rem(row, 2)
    y = lax.rem(row // 2, NY)
    z = row // (2 * NY)

    def rid(zz, yy, cc):
        return (lax.rem(zz, NZ) * NY + lax.rem(yy, NY)) * 2 + cc

    sib = rid(z, y, 1 - core)
    peers = {
        ("y", 1): rid(z, y + 1, core),
        ("y", -1): rid(z, y + NY - 1, core),
        ("z", 1): rid(z + 1, y, core),
        ("z", -1): rid(z + NZ - 1, y, core),
    }
    fills = [(dens, dg.at[row]), (occ, eo.at[row]), (own_h, em.at[row, pl.ds(0, 2)]),
             (mu_h, em.at[row, pl.ds(2, 2)]), (nu_h, em.at[row, pl.ds(4, 2)]), (slen_h, slen)]
    fills = [pltpu.make_async_copy(src, dst, in_sem.at[k]) for k, (src, dst) in enumerate(fills)]
    for fill in fills:
        fill.start()

    comp_y, comp_z = packed([o[0] for o in COMPUTE]), packed([o[1] for o in COMPUTE])
    round_a, round_b = packed([o[0] for o in ROUNDS]), packed([o[1] for o in ROUNDS])
    counts = packed(COUNTS)

    def chip_of(t):
        return lax.rem(z + entry(comp_z, t), NZ) * NY + lax.rem(y + entry(comp_y, t), NY)

    def vir_copy(t):
        q = chip_of(t)
        return pltpu.make_async_copy(
            vir.at[:, pl.ds(pl.multiple_of(q * 1024, 1024), 1024)], cbuf.at[q], vir_sem.at[t])

    def start_vir(t, _):
        vir_copy(t).start()
        return 0

    barrier = pltpu.get_barrier_semaphore()
    greeted = [(p, ax) for p in peers.values()] + [(sib, ax)]
    greeted += [(row, lax.rem(ax + k, NX)) for k in range(1, NX)]
    for target in greeted:
        pl.semaphore_signal(barrier, inc=1, device_id=target, device_id_type=pl.DeviceIdType.MESH)
    acc[...] = jnp.zeros_like(acc)
    spread[...] = (iota((128, 256), 0) == iota((128, 256), 1) // PAD).astype(F32).astype(BF16)
    occf[4 * NROW] = jnp.zeros((8, 128), F32)
    for k in range(4):
        col = iota((128, 256), 1)
        repeat[k] = (iota((128, 256), 0) == (2 * k + col // 128) * PAD + col % PAD).astype(F32).astype(BF16)
    for fill in fills:
        fill.wait()
    pl.semaphore_wait(barrier, len(greeted))

    def gather(units, compute, before):
        def send(k, r, target):
            ref_of, sem, recv, _, _ = units[k]
            pltpu.make_async_remote_copy(
                ref_of(r), ref_of(r), sem, recv.at[r],
                device_id=(target, ax), device_id_type=pl.DeviceIdType.MESH).start()

        def wait(k, r):
            ref_of, sem, recv, _, _ = units[k]
            pltpu.make_async_remote_copy(
                ref_of(r), ref_of(r), sem, recv.at[r],
                device_id=(sib, ax), device_id_type=pl.DeviceIdType.MESH).wait_recv()

        other = {"y": "z", "z": "y"}
        n = len(units)
        for phase in range(2):
            for k in range(n):
                axis = units[k][3] if phase == 0 else other[units[k][3]]
                send(k, row, peers[(axis, 1)])
                send(k, row, peers[(axis, -1)])
        for k in range(n):
            send(k, row, sib)
        before()

        def step(t, done):
            a, b = entry(round_a, t), entry(round_b, t)
            for k in range(n):
                axis, sgn = units[k][3], units[k][4]
                if sgn == 1:
                    du, dv = a, b
                else:
                    du, dv = jnp.where(b == 0, lax.rem(4 - a, 4), a), lax.rem(4 - b, 4)
                dy, dz = (du, dv) if axis == "y" else (dv, du)
                r = rid(z + dz, y + dy, core)
                wait(k, r)

                @pl.when((a == 3) & (b == 0))
                def _():
                    send(k, r, peers[(axis, sgn)])

                @pl.when(b == 0)
                def _():
                    send(k, r, peers[(other[axis], 1)])
                    send(k, r, peers[(other[axis], -1)])

                @pl.when(b == 3)
                def _():
                    send(k, r, peers[(other[axis], sgn)])

                send(k, r, sib)

            def one(c, _):
                q = chip_of(c)
                for k in range(n):
                    wait(k, q * 2 + 1 - core)
                compute(c, q)
                return 0

            last = done + entry(counts, t)
            lax.fori_loop(done, last, one, 0)
            return last

        lax.fori_loop(0, NCHIP - 1, step, jnp.int32(0))

    def rows_of(buf, k):
        return lambda r: buf.at[r, pl.ds(64 * k, 64)]

    shape_of = [("y", 1), ("z", 1), ("y", -1), ("z", -1)]
    d_units = [(rows_of(dg, k), d_send.at[k], d_recv.at[k]) + shape_of[k] for k in range(UNITS)]
    d_units.append((lambda r: eo.at[r], o_send.at[0], o_recv, "y", 1))
    d_units.append((lambda r: em.at[r], m_send.at[0], m_recv, "z", 1))
    h_units = [(rows_of(hg, k), h_send.at[k], h_recv.at[k]) + shape_of[k] for k in range(UNITS)]

    def before_d():
        lax.fori_loop(0, NCHIP, start_vir, 0)

    def compute_d(t, q):
        vir_copy(t).wait()
        part = dot_nt(dg[2 * q], cbuf[q, :, 0:512]) + dot_nt(dg[2 * q + 1], cbuf[q, :, 512:1024])
        for b in range(4):
            acc[b] += part[:, 128 * b:128 * b + 128]

    gather(d_units, compute_d, before_d)

    for i in range(OCC):
        for b in range(4):
            hg[row, 32 * i:32 * i + 32, 128 * b:128 * b + 128] = acc[b, pl.ds(i, 32, stride=OCC), :].astype(BF16)

    def before_h():
        lens = slen[...]
        lens_f = lens.astype(F32)
        lower = (iota((64, 64), 0) < iota((64, 64), 1)).astype(F32).astype(BF16)
        starts = dot(lens_f.astype(BF16), lower)
        starts_i = starts.astype(I32)
        tile = iota((NROW, 64), 0) * 4 + (starts_i >> 7)
        vtab[0:NROW, 0:64] = tile | ((starts_i & 127) << 7) | (lens << 14)
        vtab[NROW:NROW + 8, :] = jnp.zeros((8, 128), I32)
        meta = em[...]
        own = jnp.concatenate([meta[:, 0, :], meta[:, 1, :]], axis=1)
        mu = jnp.concatenate([meta[:, 2, :], meta[:, 3, :]], axis=1)
        nu = jnp.concatenate([meta[:, 4, :], meta[:, 5, :]], axis=1)
        match = own == row
        upper = (iota((256, 256), 0) < iota((256, 256), 1)).astype(F32).astype(BF16)
        rank = dot(match.astype(F32).astype(BF16), upper)
        code = ((mu - 64 * NROW) * 64 + nu).astype(F32)
        lane = iota((NROW, 128), 1)
        table = jnp.zeros((NROW, 128), F32)
        for r in range(CAP):
            val = jnp.sum(jnp.where(match & (rank == float(r)), code, 0.0), axis=1, keepdims=True)
            table = jnp.where(lane == r, val, table)
        table = table.astype(I32) + 64 * 64 * NROW
        wtab[...] = table >> 6
        c0 = pltpu.make_async_copy(vtab, stab, t_sem.at[0])
        c1 = pltpu.make_async_copy(wtab, ptab, t_sem.at[1])
        c0.start()
        c1.start()
        live = table < 64 * 64 * NROW
        nus = table & 63
        words = jnp.concatenate([starts_i * 32 + lens, jnp.zeros((NROW, 64), I32)], axis=1)
        word = jnp.where(live, jnp.take_along_axis(words, nus, axis=1), 0)
        n0i = word >> 5
        nl = word & 31
        parts = [n0i >> 6, n0i & 63, nl]
        hi, lo, ln = [dot(p.astype(F32).astype(BF16), spread[...]) for p in parts]
        inner = (iota((NROW, 256), 1) & (PAD - 1)).astype(F32)
        targets[...] = jnp.where(inner < ln, hi * 64.0 + lo + inner, -1.0)
        for r in range(NROW):
            piece = eo[r].astype(F32)
            for b in range(4):
                occf[4 * r + b] = piece[:, 128 * b:128 * b + 128]
        c0.wait()
        c1.wait()
        lane8 = iota((8, 128), 1)

        def coeffs(j, _):
            for r in range(CAP):
                g = ptab[j, r]
                w = stab[jnp.minimum((g >> 6) & 63, NROW), g & 63]
                tile = w & 127
                off = (w >> 7) & 127
                shift = (128 - off) & 127
                left = pltpu.roll(occf[tile], shift, 1)
                right = pltpu.roll(occf[tile + 1], shift, 1)
                both = jnp.where(lane8 < 128 - off, left, right)
                rolled[8 * r:8 * r + 8, :] = jnp.where(lane8 < (w >> 14), both, 0.0)
            cexp[j] = dot(rolled[...].astype(BF16), spread[...])
            return 0

        lax.fori_loop(0, NROW, coeffs, 0)

    def blocks(j):
        select = (iota((512, 256), 0).astype(F32) == targets[pl.ds(j, 1), :]).astype(F32).astype(BF16)
        tiles = dot(hg[j], select)
        tiles = tiles.astype(BF16)
        for pair in range(CAP // 2):
            g = pair // 4
            wide_tile = dot(tiles[:, 128 * g:128 * g + 128], repeat[pair % 4])
            for s in range(2):
                slot = 2 * pair + s
                acc0 = acc1 = None
                for i in range(OCC):
                    tile = wide_tile[32 * i:32 * i + 32, 128 * s:128 * s + 128]
                    row_c = cexp[j, OCC * slot + i:OCC * slot + i + 1, :]
                    t0, t1 = tile * row_c[:, 0:128], tile * row_c[:, 128:256]
                    acc0 = t0 if i == 0 else acc0 + t0
                    acc1 = t1 if i == 0 else acc1 + t1
                sq = None
                for h, part in enumerate((acc0, acc1)):
                    block = part.astype(BF16)
                    out[j * CAP + slot, :, 128 * h:128 * h + 128] = block
                    wide = block.astype(F32)
                    sq = wide * wide if h == 0 else sq + wide * wide
                squares[j, slot:slot + 1, :] = jnp.sum(sq, axis=0, keepdims=True)

    def compute_h(t, q):
        for c in range(2):
            blocks(2 * q + c)

    gather(h_units, compute_h, before_h)

    diag = iota((128, 128), 0) == iota((128, 128), 1)
    for b in range(4):
        part = squares[8 * b:8 * b + 8].reshape(128, 128)
        lanes = jnp.sum(part, axis=1, keepdims=True)
        sumout[b:b + 1, :] = jnp.sum(jnp.where(diag, lanes, 0.0), axis=0, keepdims=True)
    sumout[4:8, :] = jnp.zeros((4, 128), F32)
    sumbuf[ax] = sumout[...]
    copies = []
    for k in range(1, NX):
        peer = lax.rem(ax + k, NX)
        copy = pltpu.make_async_remote_copy(
            sumout, sumbuf.at[ax], x_send.at[k], x_recv.at[k],
            device_id=(row, peer), device_id_type=pl.DeviceIdType.MESH)
        copy.start()
        copies.append(copy)
    for k in range(UNITS):
        for buf, sem in ((dg, d_send), (hg, h_send)):
            ref = buf.at[pl.ds(0, 31), pl.ds(64 * k, 64)]
            pltpu.make_async_copy(ref, ref, sem.at[k]).wait()
    for buf, sem in ((eo, o_send), (em, m_send)):
        ref = buf.at[pl.ds(0, 31)]
        pltpu.make_async_copy(ref, ref, sem.at[0]).wait()
    for copy in copies:
        copy.wait_recv()
    total_out[...] = (sumbuf[0] + sumbuf[1]) + (sumbuf[2] + sumbuf[3])
    for copy in copies:
        copy.wait_send()


def per_device(density, vir_coeffs, occ_coeffs, shell_len, mu_shell, nu_shell, owner):
    hbm = pl.BlockSpec(memory_space=pl.ANY)
    vmem = pl.BlockSpec(memory_space=pltpu.VMEM)
    dma = pltpu.SemaphoreType.DMA
    blocks, total = pl.pallas_call(
        kernel,
        out_shape=(pltpu.VMEM((512, 32, 256), BF16), pltpu.VMEM((8, 128), F32)),
        in_specs=[hbm] * 7,
        out_specs=(vmem, vmem),
        scratch_shapes=[
            pltpu.VMEM((NROW, 256, 512), BF16),
            pltpu.VMEM((NROW, 256, 512), BF16),
            pltpu.VMEM((NCHIP, 512, 1024), BF16),
            pltpu.VMEM((NROW, 8, 512), BF16),
            pltpu.VMEM((NROW, 8, 128), I32),
            pltpu.VMEM((NROW, 64), I32),
            pltpu.VMEM((4, 256, 128), F32),
            pltpu.VMEM((4 * NROW + 1, 8, 128), F32),
            pltpu.VMEM((128, 256), BF16),
            pltpu.VMEM((4, 128, 256), BF16),
            pltpu.VMEM((128, 128), F32),
            pltpu.VMEM((NROW, 128, 256), F32),
            pltpu.VMEM((NROW, 256), F32),
            pltpu.VMEM((NROW, CAP, 128), F32),
            pltpu.VMEM((NX, 8, 128), F32),
            pltpu.VMEM((8, 128), F32),
            pltpu.VMEM((NROW + 8, 128), I32),
            pltpu.VMEM((NROW, 128), I32),
            pltpu.SMEM((NROW + 8, 128), I32),
            pltpu.SMEM((NROW, 128), I32),
            dma((6,)), dma((NCHIP,)), dma((UNITS, NROW)), dma((UNITS, NROW)), dma((NROW,)), dma((NROW,)),
            dma((UNITS,)), dma((UNITS,)), dma((1,)), dma((1,)), dma((NX,)), dma((NX,)), dma((2,)),
        ],
        compiler_params=pltpu.CompilerParams(
            collective_id=0, has_side_effects=True, vmem_limit_bytes=48 * 1024 * 1024),
    )(density.reshape(256, 512), vir_coeffs, occ_coeffs, shell_len,
      mu_shell.reshape(2, 128), nu_shell.reshape(2, 128), owner.reshape(2, 128))
    pair_scale = jnp.sqrt(total[0:4].reshape(512) / (128 * PAD * PAD) + 1e-06)
    return blocks, pair_scale


def solution(mesh):
    return jax.shard_map(
        per_device,
        mesh=mesh,
        in_specs=(
            P("aux", None, "rows"),
            P("rows", None),
            P(None, "rows"),
            P(),
            P("rows"),
            P("rows"),
            P("rows", None),
        ),
        out_specs=(P("rows", "aux", None), P("rows")),
        check_vma=False,
    )
```

```python
import jax
import jax.numpy as jnp
from jax import lax
from jax.experimental import pallas as pl
from jax.experimental.pallas import tpu as pltpu
from jax.sharding import PartitionSpec as P

NY = 4
NZ = 4
NCHIP = NY * NZ
NROW = 2 * NCHIP
NX = 4
UNITS = 4
OCC = 8
PAD = 16
CAP = 16
F32 = jnp.float32
BF16 = jnp.bfloat16
I32 = jnp.int32
ROUNDS = [(3, 0), (1, 0), (0, 3), (0, 1), (2, 0), (3, 3), (3, 1), (1, 3), (1, 1), (0, 2), (2, 3), (2, 1), (3, 2), (1, 2), (2, 2)]
COMPUTE = [(0, 0), (1, 0), (3, 0), (0, 1), (0, 3), (3, 3), (1, 1), (3, 1), (1, 3), (2, 0), (0, 2), (3, 2), (2, 3), (1, 2), (2, 1), (2, 2)]
COUNTS_D = [1, 0, 0, 0, 0, 0, 0, 0, 0, 3, 2, 3, 2, 2, 3]
COUNTS_H = [1, 0, 0, 0, 1, 1, 1, 1, 1, 1, 1, 1, 1, 1, 5]
E_COUNT = [0, 0, 0, 0, 4, 0, 0, 0, 6, 0, 0, 0, 4, 0, 0]
E_FROM = [0, 0, 0, 0, 0, 0, 0, 0, 4, 0, 0, 0, 10, 0, 0]


def pick(t, values):
    out = jnp.int32(values[0])
    for k in range(1, len(values)):
        if values[k] != values[0]:
            out = jnp.where(t == k, jnp.int32(values[k]), out)
    return out


def iota(shape, dim):
    return lax.broadcasted_iota(I32, shape, dim)


def dot(a, b):
    return lax.dot_general(a, b, (((1,), (0,)), ((), ())), preferred_element_type=F32)


def dot_nt(a, b):
    return lax.dot_general(a, b, (((1,), (1,)), ((), ())), preferred_element_type=F32)


def packed(values, bits=2):
    word = 0
    for k, v in enumerate(values):
        word |= (v % (1 << bits)) << (bits * k)
    return jnp.int32(word - (1 << 32) if word >= 1 << 31 else word)


def entry(word, t, bits=2):
    return lax.shift_right_logical(word, bits * t) & ((1 << bits) - 1)


def kernel(dens, vir, occ, slen_h, mu_h, nu_h, own_h, out, total_out,
           dg, hg, cbuf, eo, em, slen, acc, occf, spread, lined, cexp, targets, squares, sumbuf, sumout, vtab, wtab,
           stab, ptab,
           in_sem, vir_sem, d_recv, h_recv, o_recv, m_recv, d_send, h_send, o_send, m_send, x_recv, x_send, t_sem):
    row = lax.axis_index("rows")
    ax = lax.axis_index("aux")
    core = lax.rem(row, 2)
    y = lax.rem(row // 2, NY)
    z = row // (2 * NY)

    def rid(zz, yy, cc):
        return (lax.rem(zz, NZ) * NY + lax.rem(yy, NY)) * 2 + cc

    sib = rid(z, y, 1 - core)
    peers = {
        ("y", 1): rid(z, y + 1, core),
        ("y", -1): rid(z, y + NY - 1, core),
        ("z", 1): rid(z + 1, y, core),
        ("z", -1): rid(z + NZ - 1, y, core),
    }
    fills = [(dens, dg.at[row]), (occ, eo.at[row]), (own_h, em.at[row, pl.ds(0, 2)]),
             (mu_h, em.at[row, pl.ds(2, 2)]), (nu_h, em.at[row, pl.ds(4, 2)]), (slen_h, slen)]
    fills = [pltpu.make_async_copy(src, dst, in_sem.at[k]) for k, (src, dst) in enumerate(fills)]
    for fill in fills:
        fill.start()

    comp_y, comp_z = packed([o[0] for o in COMPUTE]), packed([o[1] for o in COMPUTE])
    round_a, round_b = packed([o[0] for o in ROUNDS]), packed([o[1] for o in ROUNDS])

    def chip_of(t):
        return lax.rem(z + entry(comp_z, t), NZ) * NY + lax.rem(y + entry(comp_y, t), NY)

    def vir_copy(t):
        q = chip_of(t)
        return pltpu.make_async_copy(
            vir.at[:, pl.ds(pl.multiple_of(q * 1024, 1024), 1024)], cbuf.at[q], vir_sem.at[t])

    def start_vir(t, _):
        vir_copy(t).start()
        return 0

    barrier = pltpu.get_barrier_semaphore()
    greeted = [(p, ax) for p in peers.values()] + [(sib, ax)]
    greeted += [(row, lax.rem(ax + k, NX)) for k in range(1, NX)]
    for target in greeted:
        pl.semaphore_signal(barrier, inc=1, device_id=target, device_id_type=pl.DeviceIdType.MESH)
    acc[...] = jnp.zeros_like(acc)
    spread[...] = (iota((128, 256), 0) == iota((128, 256), 1) // PAD).astype(F32).astype(BF16)
    for fill in fills:
        fill.wait()
    pl.semaphore_wait(barrier, len(greeted))

    other = {"y": "z", "z": "y"}

    def copy_of(unit, r, target):
        ref_of, sem, recv, _, _ = unit
        return pltpu.make_async_remote_copy(
            ref_of(r), ref_of(r), sem, recv.at[r],
            device_id=(target, ax), device_id_type=pl.DeviceIdType.MESH)

    def send(unit, r, target):
        copy_of(unit, r, target).start()

    def wait(unit, r):
        copy_of(unit, r, sib).wait_recv()

    def leave(units):
        for phase in range(2):
            for unit in units:
                axis = unit[3] if phase == 0 else other[unit[3]]
                send(unit, row, peers[(axis, 1)])
                send(unit, row, peers[(axis, -1)])
        for unit in units:
            send(unit, row, sib)

    def take(unit, t):
        a, b = entry(round_a, t), entry(round_b, t)
        axis, sgn = unit[3], unit[4]
        if sgn == 1:
            du, dv = a, b
        else:
            du, dv = jnp.where(b == 0, (4 - a) & 3, a), (4 - b) & 3
        dy, dz = (du, dv) if axis == "y" else (dv, du)
        r = rid(z + dz, y + dy, core)
        wait(unit, r)

        @pl.when((a == 3) & (b == 0))
        def _():
            send(unit, r, peers[(axis, sgn)])

        @pl.when(b == 0)
        def _():
            send(unit, r, peers[(other[axis], 1)])
            send(unit, r, peers[(other[axis], -1)])

        @pl.when(b == 3)
        def _():
            send(unit, r, peers[(other[axis], sgn)])

        send(unit, r, sib)

    def gather(units, counts, compute, at_round):
        def step(t, done):
            at_round(t)
            for unit in units:
                take(unit, t)

            def one(c, _):
                q = chip_of(c)
                for unit in units:
                    wait(unit, q * 2 + 1 - core)
                compute(c, q)
                return 0

            last = done + pick(t, counts)
            lax.fori_loop(done, last, one, 0)
            return last

        lax.fori_loop(0, NCHIP - 1, step, jnp.int32(0))

    def rows_of(buf, k):
        return lambda r: buf.at[r, pl.ds(64 * k, 64)]

    shape_of = [("y", 1), ("z", 1), ("y", -1), ("z", -1)]
    d_units = [(rows_of(dg, k), d_send.at[k], d_recv.at[k]) + shape_of[k] for k in range(UNITS)]
    e_units = [(lambda r: eo.at[r], o_send.at[0], o_recv, "y", 1), (lambda r: em.at[r], m_send.at[0], m_recv, "z", -1)]
    h_units = [(rows_of(hg, k), h_send.at[k], h_recv.at[k]) + shape_of[k] for k in range(UNITS)]

    def compute_d(t, q):
        vir_copy(t).wait()
        part = dot_nt(dg[2 * q], cbuf[q, :, 0:512]) + dot_nt(dg[2 * q + 1], cbuf[q, :, 512:1024])
        for b in range(4):
            acc[b] += part[:, 128 * b:128 * b + 128]

    def tables():
        for q in range(NCHIP):
            for unit in e_units:
                wait(unit, 2 * q + 1 - core)
        lens = slen[...]
        lens_f = lens.astype(F32)
        lower = (iota((64, 64), 0) < iota((64, 64), 1)).astype(F32).astype(BF16)
        starts = dot(lens_f.astype(BF16), lower)
        starts_i = starts.astype(I32)
        tile = iota((NROW, 64), 0) * 8 + (starts_i >> 6)
        vtab[0:NROW, 0:64] = tile | (((128 - (starts_i & 63)) & 127) << 8) | (lens << 16)
        vtab[NROW:64, :] = jnp.zeros((64 - NROW, 128), I32)
        meta = em[...]
        own = jnp.concatenate([meta[:, 0, :], meta[:, 1, :]], axis=1)
        mu = jnp.concatenate([meta[:, 2, :], meta[:, 3, :]], axis=1)
        nu = jnp.concatenate([meta[:, 4, :], meta[:, 5, :]], axis=1)
        match = own == row
        upper = (iota((256, 256), 0) < iota((256, 256), 1)).astype(F32).astype(BF16)
        rank = dot(match.astype(F32).astype(BF16), upper)
        code = ((mu - 64 * NROW) * 64 + nu).astype(F32)
        lane = iota((NROW, 128), 1)
        table = jnp.zeros((NROW, 128), F32)
        for r in range(CAP):
            val = jnp.sum(jnp.where(match & (rank == float(r)), code, 0.0), axis=1, keepdims=True)
            table = jnp.where(lane == r, val, table)
        table = table.astype(I32) + 64 * 64 * NROW
        wtab[...] = ((table >> 12) << 7) | ((table >> 6) & 63)
        c0 = pltpu.make_async_copy(vtab, stab, t_sem.at[0])
        c1 = pltpu.make_async_copy(wtab, ptab, t_sem.at[1])
        c0.start()
        c1.start()
        live = table < 64 * 64 * NROW
        nus = table & 63
        words = jnp.concatenate([starts_i * 32 + lens, jnp.zeros((NROW, 64), I32)], axis=1)
        word = jnp.where(live, jnp.take_along_axis(words, nus, axis=1), 0)
        n0i = word >> 5
        nl = word & 31
        parts = [n0i >> 6, n0i & 63, nl]
        hi, lo, ln = [dot(p.astype(F32).astype(BF16), spread[...]) for p in parts]
        inner = (iota((NROW, 256), 1) & (PAD - 1)).astype(F32)
        targets[...] = jnp.where(inner < ln, hi * 64.0 + lo + inner, -1.0)
        low64 = iota((8, 128), 1) < 64
        for r in range(NROW):
            piece = eo[r].astype(F32)
            parts = [piece[:, 128 * b:128 * b + 128] for b in range(4)]
            turned = [pltpu.roll(part, 64, 1) for part in parts]
            for b in range(4):
                occf[8 * r + 2 * b] = parts[b]
                occf[8 * r + 2 * b + 1] = jnp.where(low64, turned[b], turned[b + 1] if b < 3 else 0.0)
        c0.wait()
        c1.wait()

    def coeff_rows():
        lane8 = iota((8, 128), 1)
        inner8 = lane8 & (PAD - 1)
        group8 = lane8 >> 4

        def coeffs(j, _):
            for g in range(2):
                line = jnp.zeros((8, 128), F32)
                for s in range(8):
                    pair = ptab[j, 8 * g + s]
                    w = stab[(pair >> 7) & 63, pair & 127]
                    shift = ((w >> 8) + PAD * s) & 127
                    tile = pltpu.roll(occf[w & 255], shift, 1)
                    line = jnp.where((group8 == s) & (inner8 < (w >> 16)), tile, line)
                lined[pl.ds(pl.multiple_of(8 * j, 8), 8), 128 * g:128 * g + 128] = line
            return 0

        lax.fori_loop(0, NROW, coeffs, 0)

    def expand_rows():
        lined_b = lined[...].astype(BF16)
        row256, col256 = iota((256, 256), 0), iota((256, 256), 1)
        same_slot = (row256 >> 4) == (col256 >> 4)

        def expand(n, _):
            for m in range(4):
                pick_m = (same_slot & ((row256 & (PAD - 1)) == 4 * n + m)).astype(F32).astype(BF16)
                cexp[4 * n + m] = dot(lined_b, pick_m).reshape(NROW, OCC, 256)
            return 0

        lax.fori_loop(0, PAD // 4, expand, 0)

    def round_d(t):
        lo = pick(t, E_FROM)

        def extra(e, _):
            for unit in e_units:
                take(unit, e)
            return 0

        lax.fori_loop(lo, lo + pick(t, E_COUNT), extra, 0)

    leave(d_units)
    leave(e_units)
    lax.fori_loop(0, NCHIP, start_vir, 0)
    gather(d_units, COUNTS_D, compute_d, round_d)

    for i in range(OCC):
        for b in range(4):
            hg[row, 32 * i:32 * i + 32, 128 * b:128 * b + 128] = acc[b, pl.ds(i, 32, stride=OCC), :].astype(BF16)

    leave(h_units)
    for unit in e_units:
        take(unit, NCHIP - 2)
    tables()
    coeff_rows()
    expand_rows()

    def blocks(j):
        select = (iota((512, 256), 0).astype(F32) == targets[pl.ds(j, 1), :]).astype(F32).astype(BF16)
        tiles = dot(hg[j], select)
        lane = iota((32, 128), 1)
        for g in range(2):
            xs = [tiles[32 * i:32 * i + 32, 128 * g:128 * g + 128] for i in range(OCC)]
            sq = jnp.zeros((8, 128), F32)
            for h in range(2):
                ys = []
                for m in range(8 * h, 8 * h + 8):
                    part = None
                    for i in range(OCC):
                        term = xs[i] * cexp[m, j, i:i + 1, 128 * g:128 * g + 128]
                        part = term if i == 0 else part + term
                    block = part.astype(BF16)
                    wide = block.astype(F32)
                    for k in range(4):
                        piece = wide[8 * k:8 * k + 8]
                        sq = sq + piece * piece
                    ys.append(block)
                for bit in (1, 2, 4):
                    low = ((lane >> 4) & bit) == 0
                    zs = list(ys)
                    for i in range(8):
                        if i & bit:
                            continue
                        a, c = ys[i], ys[i | bit]
                        zs[i] = jnp.where(low, a, pltpu.roll(c, PAD * bit, 1))
                        zs[i | bit] = jnp.where(low, pltpu.roll(a, 128 - PAD * bit, 1), c)
                    ys = zs
                for s in range(8):
                    out[j * CAP + 8 * g + s, :, 128 * h:128 * h + 128] = ys[s]
            squares[j, :, 128 * g:128 * g + 128] = sq

    def compute_h(t, q):
        for c in range(2):
            blocks(2 * q + c)

    gather(h_units, COUNTS_H, compute_h, lambda t: None)

    total = jnp.sum(squares[...], axis=1)
    group = (iota((256, 128), 0) >> 4) == iota((256, 128), 1)
    sumout[...] = lax.dot_general(total, group.astype(F32), (((1,), (0,)), ((), ())),
                                  precision=lax.Precision.HIGHEST, preferred_element_type=F32)
    sumbuf[ax] = sumout[...]
    copies = []
    for k in range(1, NX):
        peer = lax.rem(ax + k, NX)
        copy = pltpu.make_async_remote_copy(
            sumout, sumbuf.at[ax], x_send.at[k], x_recv.at[k],
            device_id=(row, peer), device_id_type=pl.DeviceIdType.MESH)
        copy.start()
        copies.append(copy)
    for k in range(UNITS):
        for buf, sem in ((dg, d_send), (hg, h_send)):
            ref = buf.at[pl.ds(0, 31), pl.ds(64 * k, 64)]
            pltpu.make_async_copy(ref, ref, sem.at[k]).wait()
    for buf, sem in ((eo, o_send), (em, m_send)):
        ref = buf.at[pl.ds(0, 31)]
        pltpu.make_async_copy(ref, ref, sem.at[0]).wait()
    for copy in copies:
        copy.wait_recv()
    total_out[...] = (sumbuf[0] + sumbuf[1]) + (sumbuf[2] + sumbuf[3])
    for copy in copies:
        copy.wait_send()


def per_device(density, vir_coeffs, occ_coeffs, shell_len, mu_shell, nu_shell, owner):
    hbm = pl.BlockSpec(memory_space=pl.ANY)
    vmem = pl.BlockSpec(memory_space=pltpu.VMEM)
    dma = pltpu.SemaphoreType.DMA
    blocks, total = pl.pallas_call(
        kernel,
        out_shape=(pltpu.VMEM((512, 32, 256), BF16), pltpu.VMEM((NROW, 128), F32)),
        in_specs=[hbm] * 7,
        out_specs=(vmem, vmem),
        scratch_shapes=[
            pltpu.VMEM((NROW, 256, 512), BF16),
            pltpu.VMEM((NROW, 256, 512), BF16),
            pltpu.VMEM((NCHIP, 512, 1024), BF16),
            pltpu.VMEM((NROW, 8, 512), BF16),
            pltpu.VMEM((NROW, 8, 128), I32),
            pltpu.VMEM((NROW, 64), I32),
            pltpu.VMEM((4, 256, 128), F32),
            pltpu.VMEM((8 * NROW, 8, 128), F32),
            pltpu.VMEM((128, 256), BF16),
            pltpu.VMEM((256, 256), F32),
            pltpu.VMEM((PAD, NROW, OCC, 256), F32),
            pltpu.VMEM((NROW, 256), F32),
            pltpu.VMEM((NROW, 8, 256), F32),
            pltpu.VMEM((NX, NROW, 128), F32),
            pltpu.VMEM((NROW, 128), F32),
            pltpu.VMEM((64, 128), I32),
            pltpu.VMEM((NROW, 128), I32),
            pltpu.SMEM((64, 128), I32),
            pltpu.SMEM((NROW, 128), I32),
            dma((6,)), dma((NCHIP,)), dma((UNITS, NROW)), dma((UNITS, NROW)), dma((NROW,)), dma((NROW,)),
            dma((UNITS,)), dma((UNITS,)), dma((1,)), dma((1,)), dma((NX,)), dma((NX,)), dma((2,)),
        ],
        compiler_params=pltpu.CompilerParams(
            collective_id=0, has_side_effects=True, vmem_limit_bytes=48 * 1024 * 1024),
    )(density.reshape(256, 512), vir_coeffs, occ_coeffs, shell_len,
      mu_shell.reshape(2, 128), nu_shell.reshape(2, 128), owner.reshape(2, 128))
    pair_scale = jnp.sqrt(total[:, :CAP].reshape(512) / (128 * PAD * PAD) + 1e-06)
    return blocks, pair_scale


def solution(mesh):
    return jax.shard_map(
        per_device,
        mesh=mesh,
        in_specs=(
            P("aux", None, "rows"),
            P("rows", None),
            P(None, "rows"),
            P(),
            P("rows"),
            P("rows"),
            P("rows", None),
        ),
        out_specs=(P("rows", "aux", None), P("rows")),
        check_vma=False,
    )
```

```python
import jax
import jax.numpy as jnp
from jax import lax
from jax.experimental import pallas as pl
from jax.experimental.pallas import tpu as pltpu
from jax.sharding import PartitionSpec as P

NY = 4
NZ = 4
NCHIP = NY * NZ
NROW = 2 * NCHIP
NX = 4
UNITS = 4
OCC = 8
PAD = 16
CAP = 16
F32 = jnp.float32
BF16 = jnp.bfloat16
I32 = jnp.int32
ROUNDS = [(3, 0), (1, 0), (0, 3), (0, 1), (2, 0), (3, 3), (3, 1), (1, 3), (1, 1), (0, 2), (2, 3), (2, 1), (3, 2), (1, 2), (2, 2)]
COMPUTE = [(0, 0), (1, 0), (3, 0), (0, 1), (0, 3), (3, 3), (1, 1), (3, 1), (1, 3), (2, 0), (0, 2), (3, 2), (2, 3), (1, 2), (2, 1), (2, 2)]
COUNTS_D = [1, 0, 0, 0, 0, 0, 0, 0, 0, 3, 2, 3, 2, 2, 3]
COUNTS_H = [1, 0, 0, 0, 1, 1, 1, 1, 1, 1, 1, 1, 1, 1, 5]
E_COUNT = [0, 0, 0, 0, 4, 0, 0, 0, 6, 0, 0, 0, 4, 0, 0]
E_FROM = [0, 0, 0, 0, 0, 0, 0, 0, 4, 0, 0, 0, 10, 0, 0]


def pick(t, values):
    out = jnp.int32(values[0])
    for k in range(1, len(values)):
        if values[k] != values[0]:
            out = jnp.where(t == k, jnp.int32(values[k]), out)
    return out


def iota(shape, dim):
    return lax.broadcasted_iota(I32, shape, dim)


def dot(a, b):
    return lax.dot_general(a, b, (((1,), (0,)), ((), ())), preferred_element_type=F32)


def dot_nt(a, b):
    return lax.dot_general(a, b, (((1,), (1,)), ((), ())), preferred_element_type=F32)


def packed(values, bits=2):
    word = 0
    for k, v in enumerate(values):
        word |= (v % (1 << bits)) << (bits * k)
    return jnp.int32(word - (1 << 32) if word >= 1 << 31 else word)


def entry(word, t, bits=2):
    return lax.shift_right_logical(word, bits * t) & ((1 << bits) - 1)


def kernel(dens, vir, occ, slen_h, mu_h, nu_h, own_h, out, total_out,
           dg, hg, cbuf, eo, em, slen, acc, occf, spread, lined, cexp, targets, squares, sumbuf, sumout, vtab, wtab,
           stab, ptab,
           in_sem, vir_sem, d_recv, h_recv, o_recv, m_recv, d_send, h_send, o_send, m_send, x_recv, x_send, t_sem):
    row = lax.axis_index("rows")
    ax = lax.axis_index("aux")
    core = lax.rem(row, 2)
    y = lax.rem(row // 2, NY)
    z = row // (2 * NY)

    def rid(zz, yy, cc):
        return (lax.rem(zz, NZ) * NY + lax.rem(yy, NY)) * 2 + cc

    sib = rid(z, y, 1 - core)
    peers = {
        ("y", 1): rid(z, y + 1, core),
        ("y", -1): rid(z, y + NY - 1, core),
        ("z", 1): rid(z + 1, y, core),
        ("z", -1): rid(z + NZ - 1, y, core),
    }
    fills = [(dens, dg.at[row]), (occ, eo.at[row]), (own_h, em.at[row, pl.ds(0, 2)]),
             (mu_h, em.at[row, pl.ds(2, 2)]), (nu_h, em.at[row, pl.ds(4, 2)]), (slen_h, slen)]
    fills = [pltpu.make_async_copy(src, dst, in_sem.at[k]) for k, (src, dst) in enumerate(fills)]
    for fill in fills:
        fill.start()

    comp_y, comp_z = packed([o[0] for o in COMPUTE]), packed([o[1] for o in COMPUTE])
    round_a, round_b = packed([o[0] for o in ROUNDS]), packed([o[1] for o in ROUNDS])

    def chip_of(t):
        return lax.rem(z + entry(comp_z, t), NZ) * NY + lax.rem(y + entry(comp_y, t), NY)

    def vir_copy(t):
        q = chip_of(t)
        return pltpu.make_async_copy(
            vir.at[:, pl.ds(pl.multiple_of(q * 1024, 1024), 1024)], cbuf.at[q], vir_sem.at[t])

    def start_vir(t, _):
        vir_copy(t).start()
        return 0

    barrier = pltpu.get_barrier_semaphore()
    greeted = [(p, ax) for p in peers.values()] + [(sib, ax)]
    greeted += [(row, lax.rem(ax + k, NX)) for k in range(1, NX)]
    for target in greeted:
        pl.semaphore_signal(barrier, inc=1, device_id=target, device_id_type=pl.DeviceIdType.MESH)
    acc[...] = jnp.zeros_like(acc)
    spread[...] = (iota((128, 256), 0) == iota((128, 256), 1) // PAD).astype(F32).astype(BF16)
    for fill in fills:
        fill.wait()
    pl.semaphore_wait(barrier, len(greeted))

    other = {"y": "z", "z": "y"}

    def copy_of(unit, r, target):
        ref_of, sem, recv, _, _ = unit
        return pltpu.make_async_remote_copy(
            ref_of(r), ref_of(r), sem, recv.at[r],
            device_id=(target, ax), device_id_type=pl.DeviceIdType.MESH)

    def send(unit, r, target):
        copy_of(unit, r, target).start()

    def wait(unit, r):
        copy_of(unit, r, sib).wait_recv()

    def leave(units):
        for phase in range(2):
            for unit in units:
                axis = unit[3] if phase == 0 else other[unit[3]]
                send(unit, row, peers[(axis, 1)])
                send(unit, row, peers[(axis, -1)])
        for unit in units:
            send(unit, row, sib)

    def take(unit, t):
        a, b = entry(round_a, t), entry(round_b, t)
        axis, sgn = unit[3], unit[4]
        if sgn == 1:
            du, dv = a, b
        else:
            du, dv = jnp.where(b == 0, (4 - a) & 3, a), (4 - b) & 3
        dy, dz = (du, dv) if axis == "y" else (dv, du)
        r = rid(z + dz, y + dy, core)
        wait(unit, r)

        @pl.when((a == 3) & (b == 0))
        def _():
            send(unit, r, peers[(axis, sgn)])

        @pl.when(b == 0)
        def _():
            send(unit, r, peers[(other[axis], 1)])
            send(unit, r, peers[(other[axis], -1)])

        @pl.when(b == 3)
        def _():
            send(unit, r, peers[(other[axis], sgn)])

        send(unit, r, sib)

    def gather(units, counts, compute, at_round):
        def step(t, done):
            at_round(t)
            for unit in units:
                take(unit, t)

            def one(c, _):
                q = chip_of(c)
                for unit in units:
                    wait(unit, q * 2 + 1 - core)
                compute(c, q)
                return 0

            last = done + pick(t, counts)
            lax.fori_loop(done, last, one, 0)
            return last

        lax.fori_loop(0, NCHIP - 1, step, jnp.int32(0))

    def rows_of(buf, k):
        return lambda r: buf.at[r, pl.ds(64 * k, 64)]

    shape_of = [("y", 1), ("z", 1), ("y", -1), ("z", -1)]
    d_units = [(rows_of(dg, k), d_send.at[k], d_recv.at[k]) + shape_of[k] for k in range(UNITS)]
    e_units = [(lambda r: eo.at[r], o_send.at[0], o_recv, "y", 1), (lambda r: em.at[r], m_send.at[0], m_recv, "z", -1)]
    h_units = [(rows_of(hg, k), h_send.at[k], h_recv.at[k]) + shape_of[k] for k in range(UNITS)]

    def compute_d(t, q):
        vir_copy(t).wait()
        part = dot_nt(dg[2 * q], cbuf[q, :, 0:512]) + dot_nt(dg[2 * q + 1], cbuf[q, :, 512:1024])
        for b in range(4):
            acc[b] += part[:, 128 * b:128 * b + 128]

    def tables():
        for q in range(NCHIP):
            for unit in e_units:
                wait(unit, 2 * q + 1 - core)
        lens = slen[...]
        lens_f = lens.astype(F32)
        lower = (iota((64, 64), 0) < iota((64, 64), 1)).astype(F32).astype(BF16)
        starts = dot(lens_f.astype(BF16), lower)
        starts_i = starts.astype(I32)
        tile = iota((NROW, 64), 0) * 8 + (starts_i >> 6)
        vtab[0:NROW, 0:64] = tile | (((128 - (starts_i & 63)) & 127) << 8) | (lens << 16)
        vtab[NROW:64, :] = jnp.zeros((64 - NROW, 128), I32)
        meta = em[...]
        own = jnp.concatenate([meta[:, 0, :], meta[:, 1, :]], axis=1)
        mu = jnp.concatenate([meta[:, 2, :], meta[:, 3, :]], axis=1)
        nu = jnp.concatenate([meta[:, 4, :], meta[:, 5, :]], axis=1)
        match = own == row
        upper = (iota((256, 256), 0) < iota((256, 256), 1)).astype(F32).astype(BF16)
        rank = dot(match.astype(F32).astype(BF16), upper)
        code = ((mu - 64 * NROW) * 64 + nu).astype(F32)
        lane = iota((NROW, 128), 1)
        table = jnp.zeros((NROW, 128), F32)
        for r in range(CAP):
            val = jnp.sum(jnp.where(match & (rank == float(r)), code, 0.0), axis=1, keepdims=True)
            table = jnp.where(lane == r, val, table)
        table = table.astype(I32) + 64 * 64 * NROW
        wtab[...] = ((table >> 12) << 7) | ((table >> 6) & 63)
        c0 = pltpu.make_async_copy(vtab, stab, t_sem.at[0])
        c1 = pltpu.make_async_copy(wtab, ptab, t_sem.at[1])
        c0.start()
        c1.start()
        live = table < 64 * 64 * NROW
        nus = table & 63
        words = jnp.concatenate([starts_i * 32 + lens, jnp.zeros((NROW, 64), I32)], axis=1)
        word = jnp.where(live, jnp.take_along_axis(words, nus, axis=1), 0)
        n0i = word >> 5
        nl = word & 31
        parts = [n0i >> 6, n0i & 63, nl]
        hi, lo, ln = [dot(p.astype(F32).astype(BF16), spread[...]) for p in parts]
        inner = (iota((NROW, 256), 1) & (PAD - 1)).astype(F32)
        targets[...] = jnp.where(inner < ln, hi * 64.0 + lo + inner, -1.0)
        low64 = iota((8, 128), 1) < 64
        for r in range(NROW):
            piece = eo[r].astype(F32)
            parts = [piece[:, 128 * b:128 * b + 128] for b in range(4)]
            turned = [pltpu.roll(part, 64, 1) for part in parts]
            for b in range(4):
                occf[8 * r + 2 * b] = parts[b]
                occf[8 * r + 2 * b + 1] = jnp.where(low64, turned[b], turned[b + 1] if b < 3 else 0.0)
        c0.wait()
        c1.wait()

    def coeff_rows():
        lane8 = iota((8, 128), 1)
        inner8 = lane8 & (PAD - 1)
        group8 = lane8 >> 4

        def coeffs(j, _):
            for g in range(2):
                line = jnp.zeros((8, 128), F32)
                for s in range(8):
                    pair = ptab[j, 8 * g + s]
                    w = stab[(pair >> 7) & 63, pair & 127]
                    shift = ((w >> 8) + PAD * s) & 127
                    tile = pltpu.roll(occf[w & 255], shift, 1)
                    line = jnp.where((group8 == s) & (inner8 < (w >> 16)), tile, line)
                lined[pl.ds(pl.multiple_of(8 * j, 8), 8), 128 * g:128 * g + 128] = line
            return 0

        lax.fori_loop(0, NROW, coeffs, 0, unroll=4)

    def expand_rows():
        lined_b = lined[...].astype(BF16)
        row256, col256 = iota((256, 256), 0), iota((256, 256), 1)
        same_slot = (row256 >> 4) == (col256 >> 4)

        def expand(n, _):
            for m in range(8):
                pick_m = (same_slot & ((row256 & (PAD - 1)) == 8 * n + m)).astype(F32).astype(BF16)
                cexp[8 * n + m] = dot(lined_b, pick_m).reshape(NROW, OCC, 256)
            return 0

        lax.fori_loop(0, PAD // 8, expand, 0)

    def round_d(t):
        lo = pick(t, E_FROM)

        def extra(e, _):
            for unit in e_units:
                take(unit, e)
            return 0

        lax.fori_loop(lo, lo + pick(t, E_COUNT), extra, 0)

    leave(d_units)
    leave(e_units)
    lax.fori_loop(0, NCHIP, start_vir, 0)
    gather(d_units, COUNTS_D, compute_d, round_d)

    for i in range(OCC):
        for b in range(4):
            hg[row, 32 * i:32 * i + 32, 128 * b:128 * b + 128] = acc[b, pl.ds(i, 32, stride=OCC), :].astype(BF16)

    leave(h_units)
    for unit in e_units:
        take(unit, NCHIP - 2)
    tables()
    coeff_rows()
    expand_rows()

    def blocks(j):
        select = (iota((512, 256), 0).astype(F32) == targets[pl.ds(j, 1), :]).astype(F32).astype(BF16)
        tiles = dot(hg[j], select)
        lane = iota((32, 128), 1)
        for g in range(2):
            xs = [tiles[32 * i:32 * i + 32, 128 * g:128 * g + 128] for i in range(OCC)]
            sq = jnp.zeros((8, 128), F32)
            for h in range(2):
                ys = []
                for m in range(8 * h, 8 * h + 8):
                    part = None
                    for i in range(OCC):
                        term = xs[i] * cexp[m, j, i:i + 1, 128 * g:128 * g + 128]
                        part = term if i == 0 else part + term
                    block = part.astype(BF16)
                    wide = block.astype(F32)
                    for k in range(4):
                        piece = wide[8 * k:8 * k + 8]
                        sq = sq + piece * piece
                    ys.append(block)
                for bit in (1, 2, 4):
                    low = ((lane >> 4) & bit) == 0
                    zs = list(ys)
                    for i in range(8):
                        if i & bit:
                            continue
                        a, c = ys[i], ys[i | bit]
                        zs[i] = jnp.where(low, a, pltpu.roll(c, PAD * bit, 1))
                        zs[i | bit] = jnp.where(low, pltpu.roll(a, 128 - PAD * bit, 1), c)
                    ys = zs
                for s in range(8):
                    out[j * CAP + 8 * g + s, :, 128 * h:128 * h + 128] = ys[s]
            squares[j, :, 128 * g:128 * g + 128] = sq

    def compute_h(t, q):
        for c in range(2):
            blocks(2 * q + c)

    gather(h_units, COUNTS_H, compute_h, lambda t: None)

    total = jnp.sum(squares[...], axis=1)
    group = (iota((256, 128), 0) >> 4) == iota((256, 128), 1)
    sumout[...] = lax.dot_general(total, group.astype(F32), (((1,), (0,)), ((), ())),
                                  precision=lax.Precision.HIGHEST, preferred_element_type=F32)
    sumbuf[ax] = sumout[...]
    copies = []
    for k in range(1, NX):
        peer = lax.rem(ax + k, NX)
        copy = pltpu.make_async_remote_copy(
            sumout, sumbuf.at[ax], x_send.at[k], x_recv.at[k],
            device_id=(row, peer), device_id_type=pl.DeviceIdType.MESH)
        copy.start()
        copies.append(copy)
    for k in range(UNITS):
        for buf, sem in ((dg, d_send), (hg, h_send)):
            ref = buf.at[pl.ds(0, 31), pl.ds(64 * k, 64)]
            pltpu.make_async_copy(ref, ref, sem.at[k]).wait()
    for buf, sem in ((eo, o_send), (em, m_send)):
        ref = buf.at[pl.ds(0, 31)]
        pltpu.make_async_copy(ref, ref, sem.at[0]).wait()
    for copy in copies:
        copy.wait_recv()
    total_out[...] = (sumbuf[0] + sumbuf[1]) + (sumbuf[2] + sumbuf[3])
    for copy in copies:
        copy.wait_send()


def per_device(density, vir_coeffs, occ_coeffs, shell_len, mu_shell, nu_shell, owner):
    hbm = pl.BlockSpec(memory_space=pl.ANY)
    vmem = pl.BlockSpec(memory_space=pltpu.VMEM)
    dma = pltpu.SemaphoreType.DMA
    blocks, total = pl.pallas_call(
        kernel,
        out_shape=(pltpu.VMEM((512, 32, 256), BF16), pltpu.VMEM((NROW, 128), F32)),
        in_specs=[hbm] * 7,
        out_specs=(vmem, vmem),
        scratch_shapes=[
            pltpu.VMEM((NROW, 256, 512), BF16),
            pltpu.VMEM((NROW, 256, 512), BF16),
            pltpu.VMEM((NCHIP, 512, 1024), BF16),
            pltpu.VMEM((NROW, 8, 512), BF16),
            pltpu.VMEM((NROW, 8, 128), I32),
            pltpu.VMEM((NROW, 64), I32),
            pltpu.VMEM((4, 256, 128), F32),
            pltpu.VMEM((8 * NROW, 8, 128), F32),
            pltpu.VMEM((128, 256), BF16),
            pltpu.VMEM((256, 256), F32),
            pltpu.VMEM((PAD, NROW, OCC, 256), F32),
            pltpu.VMEM((NROW, 256), F32),
            pltpu.VMEM((NROW, 8, 256), F32),
            pltpu.VMEM((NX, NROW, 128), F32),
            pltpu.VMEM((NROW, 128), F32),
            pltpu.VMEM((64, 128), I32),
            pltpu.VMEM((NROW, 128), I32),
            pltpu.SMEM((64, 128), I32),
            pltpu.SMEM((NROW, 128), I32),
            dma((6,)), dma((NCHIP,)), dma((UNITS, NROW)), dma((UNITS, NROW)), dma((NROW,)), dma((NROW,)),
            dma((UNITS,)), dma((UNITS,)), dma((1,)), dma((1,)), dma((NX,)), dma((NX,)), dma((2,)),
        ],
        compiler_params=pltpu.CompilerParams(
            collective_id=0, has_side_effects=True, vmem_limit_bytes=48 * 1024 * 1024),
    )(density.reshape(256, 512), vir_coeffs, occ_coeffs, shell_len,
      mu_shell.reshape(2, 128), nu_shell.reshape(2, 128), owner.reshape(2, 128))
    pair_scale = jnp.sqrt(total[:, :CAP].reshape(512) / (128 * PAD * PAD) + 1e-06)
    return blocks, pair_scale


def solution(mesh):
    return jax.shard_map(
        per_device,
        mesh=mesh,
        in_specs=(
            P("aux", None, "rows"),
            P("rows", None),
            P(None, "rows"),
            P(),
            P("rows"),
            P("rows"),
            P("rows", None),
        ),
        out_specs=(P("rows", "aux", None), P("rows")),
        check_vma=False,
    )
```

```python
import jax
import jax.numpy as jnp
from jax import lax
from jax.experimental import pallas as pl
from jax.experimental.pallas import tpu as pltpu
from jax.sharding import PartitionSpec as P

NY = 4
NZ = 4
NCHIP = NY * NZ
NROW = 2 * NCHIP
NX = 4
UNITS = 4
OCC = 8
PAD = 16
CAP = 16
F32 = jnp.float32
BF16 = jnp.bfloat16
I32 = jnp.int32
ROUNDS = [(3, 0), (1, 0), (0, 3), (0, 1), (2, 0), (3, 3), (3, 1), (1, 3), (1, 1), (0, 2), (2, 3), (2, 1), (3, 2), (1, 2), (2, 2)]
COMPUTE = [(0, 0), (1, 0), (3, 0), (0, 1), (0, 3), (3, 3), (1, 1), (3, 1), (1, 3), (2, 0), (0, 2), (3, 2), (2, 3), (1, 2), (2, 1), (2, 2)]
COUNTS_D = [1, 0, 0, 0, 0, 0, 0, 0, 0, 3, 2, 3, 2, 2, 3]
COUNTS_H = [1, 0, 0, 0, 1, 1, 1, 1, 1, 1, 1, 1, 1, 1, 5]
E_COUNT = [0, 0, 0, 0, 4, 0, 0, 0, 6, 0, 0, 0, 4, 0, 0]
E_FROM = [0, 0, 0, 0, 0, 0, 0, 0, 4, 0, 0, 0, 10, 0, 0]


def pick(t, values):
    out = jnp.int32(values[0])
    for k in range(1, len(values)):
        if values[k] != values[0]:
            out = jnp.where(t == k, jnp.int32(values[k]), out)
    return out


def iota(shape, dim):
    return lax.broadcasted_iota(I32, shape, dim)


def dot(a, b):
    return lax.dot_general(a, b, (((1,), (0,)), ((), ())), preferred_element_type=F32)


def dot_nt(a, b):
    return lax.dot_general(a, b, (((1,), (1,)), ((), ())), preferred_element_type=F32)


def packed(values, bits=2):
    word = 0
    for k, v in enumerate(values):
        word |= (v % (1 << bits)) << (bits * k)
    return jnp.int32(word - (1 << 32) if word >= 1 << 31 else word)


def entry(word, t, bits=2):
    return lax.shift_right_logical(word, bits * t) & ((1 << bits) - 1)


def kernel(dens, vir, occ, slen_h, mu_h, nu_h, own_h, out, total_out,
           dg, hg, cbuf, eo, em, slen, acc, occf, spread, lined, cexp, targets, squares, sumbuf, sumout, vtab, wtab,
           stab, ptab,
           in_sem, vir_sem, d_recv, h_recv, o_recv, m_recv, d_send, h_send, o_send, m_send, x_recv, x_send, t_sem):
    row = lax.axis_index("rows")
    ax = lax.axis_index("aux")
    core = lax.rem(row, 2)
    y = lax.rem(row // 2, NY)
    z = row // (2 * NY)

    def rid(zz, yy, cc):
        return (lax.rem(zz, NZ) * NY + lax.rem(yy, NY)) * 2 + cc

    sib = rid(z, y, 1 - core)
    peers = {
        ("y", 1): rid(z, y + 1, core),
        ("y", -1): rid(z, y + NY - 1, core),
        ("z", 1): rid(z + 1, y, core),
        ("z", -1): rid(z + NZ - 1, y, core),
    }
    fills = [(dens, dg.at[row]), (occ, eo.at[row]), (own_h, em.at[row, pl.ds(0, 2)]),
             (mu_h, em.at[row, pl.ds(2, 2)]), (nu_h, em.at[row, pl.ds(4, 2)]), (slen_h, slen)]
    fills = [pltpu.make_async_copy(src, dst, in_sem.at[k]) for k, (src, dst) in enumerate(fills)]
    for fill in fills:
        fill.start()

    comp_y, comp_z = packed([o[0] for o in COMPUTE]), packed([o[1] for o in COMPUTE])
    round_a, round_b = packed([o[0] for o in ROUNDS]), packed([o[1] for o in ROUNDS])

    def chip_of(t):
        return lax.rem(z + entry(comp_z, t), NZ) * NY + lax.rem(y + entry(comp_y, t), NY)

    def vir_copy(t):
        q = chip_of(t)
        return pltpu.make_async_copy(
            vir.at[:, pl.ds(pl.multiple_of(q * 1024, 1024), 1024)], cbuf.at[q], vir_sem.at[t])

    def start_vir(t, _):
        vir_copy(t).start()
        return 0

    barrier = pltpu.get_barrier_semaphore()
    greeted = [(p, ax) for p in peers.values()] + [(sib, ax)]
    greeted += [(row, lax.rem(ax + k, NX)) for k in range(1, NX)]
    for target in greeted:
        pl.semaphore_signal(barrier, inc=1, device_id=target, device_id_type=pl.DeviceIdType.MESH)
    acc[...] = jnp.zeros_like(acc)
    spread[...] = (iota((128, 256), 0) == iota((128, 256), 1) // PAD).astype(F32).astype(BF16)
    for fill in fills:
        fill.wait()
    pl.semaphore_wait(barrier, len(greeted))

    other = {"y": "z", "z": "y"}

    def copy_of(unit, r, target):
        ref_of, sem, recv, _, _ = unit
        return pltpu.make_async_remote_copy(
            ref_of(r), ref_of(r), sem, recv.at[r],
            device_id=(target, ax), device_id_type=pl.DeviceIdType.MESH)

    def send(unit, r, target):
        copy_of(unit, r, target).start()

    def wait(unit, r):
        copy_of(unit, r, sib).wait_recv()

    def leave(units):
        for phase in range(2):
            for unit in units:
                axis = unit[3] if phase == 0 else other[unit[3]]
                send(unit, row, peers[(axis, 1)])
                send(unit, row, peers[(axis, -1)])
        for unit in units:
            send(unit, row, sib)

    def take(unit, t):
        a, b = entry(round_a, t), entry(round_b, t)
        axis, sgn = unit[3], unit[4]
        if sgn == 1:
            du, dv = a, b
        else:
            du, dv = jnp.where(b == 0, (4 - a) & 3, a), (4 - b) & 3
        dy, dz = (du, dv) if axis == "y" else (dv, du)
        r = rid(z + dz, y + dy, core)
        wait(unit, r)

        @pl.when((a == 3) & (b == 0))
        def _():
            send(unit, r, peers[(axis, sgn)])

        @pl.when(b == 0)
        def _():
            send(unit, r, peers[(other[axis], 1)])
            send(unit, r, peers[(other[axis], -1)])

        @pl.when(b == 3)
        def _():
            send(unit, r, peers[(other[axis], sgn)])

        send(unit, r, sib)

    def gather(units, counts, compute, at_round):
        def step(t, done):
            at_round(t)
            for unit in units:
                take(unit, t)

            def one(c, _):
                q = chip_of(c)
                for unit in units:
                    wait(unit, q * 2 + 1 - core)
                compute(c, q)
                return 0

            last = done + pick(t, counts)
            lax.fori_loop(done, last, one, 0)
            return last

        lax.fori_loop(0, NCHIP - 1, step, jnp.int32(0))

    def rows_of(buf, k):
        return lambda r: buf.at[r, pl.ds(64 * k, 64)]

    shape_of = [("y", 1), ("z", 1), ("y", -1), ("z", -1)]
    d_units = [(rows_of(dg, k), d_send.at[k], d_recv.at[k]) + shape_of[k] for k in range(UNITS)]
    e_units = [(lambda r: eo.at[r], o_send.at[0], o_recv, "y", 1), (lambda r: em.at[r], m_send.at[0], m_recv, "z", -1)]
    h_units = [(rows_of(hg, k), h_send.at[k], h_recv.at[k]) + shape_of[k] for k in range(UNITS)]

    def compute_d(t, q):
        vir_copy(t).wait()
        part = dot_nt(dg[2 * q], cbuf[q, :, 0:512]) + dot_nt(dg[2 * q + 1], cbuf[q, :, 512:1024])
        for b in range(4):
            acc[b] += part[:, 128 * b:128 * b + 128]

    def tables():
        for q in range(NCHIP):
            for unit in e_units:
                wait(unit, 2 * q + 1 - core)
        lens = slen[...]
        lens_f = lens.astype(F32)
        lower = (iota((64, 64), 0) < iota((64, 64), 1)).astype(F32).astype(BF16)
        starts = dot(lens_f.astype(BF16), lower)
        starts_i = starts.astype(I32)
        tile = iota((NROW, 64), 0) * 8 + (starts_i >> 6)
        vtab[0:NROW, 0:64] = tile | (((128 - (starts_i & 63)) & 127) << 8) | (lens << 16)
        vtab[NROW:64, :] = jnp.zeros((64 - NROW, 128), I32)
        meta = em[...]
        own = jnp.concatenate([meta[:, 0, :], meta[:, 1, :]], axis=1)
        mu = jnp.concatenate([meta[:, 2, :], meta[:, 3, :]], axis=1)
        nu = jnp.concatenate([meta[:, 4, :], meta[:, 5, :]], axis=1)
        match = own == row
        upper = (iota((256, 256), 0) < iota((256, 256), 1)).astype(F32).astype(BF16)
        rank = dot(match.astype(F32).astype(BF16), upper)
        code = ((mu - 64 * NROW) * 64 + nu).astype(F32)
        lane = iota((NROW, 128), 1)
        table = jnp.zeros((NROW, 128), F32)
        for r in range(CAP):
            val = jnp.sum(jnp.where(match & (rank == float(r)), code, 0.0), axis=1, keepdims=True)
            table = jnp.where(lane == r, val, table)
        table = table.astype(I32) + 64 * 64 * NROW
        wtab[...] = ((table >> 12) << 7) | ((table >> 6) & 63)
        c0 = pltpu.make_async_copy(vtab, stab, t_sem.at[0])
        c1 = pltpu.make_async_copy(wtab, ptab, t_sem.at[1])
        c0.start()
        c1.start()
        live = table < 64 * 64 * NROW
        nus = table & 63
        words = jnp.concatenate([starts_i * 32 + lens, jnp.zeros((NROW, 64), I32)], axis=1)
        word = jnp.where(live, jnp.take_along_axis(words, nus, axis=1), 0)
        n0i = word >> 5
        nl = word & 31
        parts = [n0i >> 6, n0i & 63, nl]
        hi, lo, ln = [dot(p.astype(F32).astype(BF16), spread[...]) for p in parts]
        inner = (iota((NROW, 256), 1) & (PAD - 1)).astype(F32)
        targets[...] = jnp.where(inner < ln, hi * 64.0 + lo + inner, -1.0)
        low64 = iota((8, 128), 1) < 64
        for r in range(NROW):
            piece = eo[r].astype(F32)
            parts = [piece[:, 128 * b:128 * b + 128] for b in range(4)]
            turned = [pltpu.roll(part, 64, 1) for part in parts]
            for b in range(4):
                occf[8 * r + 2 * b] = parts[b]
                occf[8 * r + 2 * b + 1] = jnp.where(low64, turned[b], turned[b + 1] if b < 3 else 0.0)
        c0.wait()
        c1.wait()

    def coeff_rows():
        lane8 = iota((8, 128), 1)
        inner8 = lane8 & (PAD - 1)
        group8 = lane8 >> 4

        def coeffs(j, _):
            for g in range(2):
                line = jnp.zeros((8, 128), F32)
                for s in range(8):
                    pair = ptab[j, 8 * g + s]
                    w = stab[(pair >> 7) & 63, pair & 127]
                    shift = ((w >> 8) + PAD * s) & 127
                    tile = pltpu.roll(occf[w & 255], shift, 1)
                    line = jnp.where((group8 == s) & (inner8 < (w >> 16)), tile, line)
                lined[pl.ds(pl.multiple_of(8 * j, 8), 8), 128 * g:128 * g + 128] = line
            return 0

        lax.fori_loop(0, NROW, coeffs, 0, unroll=4)

    def expand_rows():
        lined_b = lined[...].astype(BF16)
        row256, col256 = iota((256, 256), 0), iota((256, 256), 1)
        same_slot = (row256 >> 4) == (col256 >> 4)

        def expand(n, _):
            for m in range(8):
                pick_m = (same_slot & ((row256 & (PAD - 1)) == 8 * n + m)).astype(F32).astype(BF16)
                cexp[8 * n + m] = dot(lined_b, pick_m).reshape(NROW, OCC, 256)
            return 0

        lax.fori_loop(0, PAD // 8, expand, 0)

    def round_d(t):
        lo = pick(t, E_FROM)

        def extra(e, _):
            for unit in e_units:
                take(unit, e)
            return 0

        lax.fori_loop(lo, lo + pick(t, E_COUNT), extra, 0)

    leave(d_units)
    leave(e_units)
    lax.fori_loop(0, NCHIP, start_vir, 0)
    gather(d_units, COUNTS_D, compute_d, round_d)

    for i in range(OCC):
        for b in range(4):
            hg[row, 32 * i:32 * i + 32, 128 * b:128 * b + 128] = acc[b, pl.ds(i, 32, stride=OCC), :].astype(BF16)

    leave(h_units)
    for unit in e_units:
        take(unit, NCHIP - 2)
    tables()
    coeff_rows()
    expand_rows()

    def blocks(j):
        select = (iota((512, 256), 0).astype(F32) == targets[pl.ds(j, 1), :]).astype(F32).astype(BF16)
        tiles = dot(hg[j], select)
        lane = iota((32, 128), 1)
        for g in range(2):
            xs = [tiles[32 * i:32 * i + 32, 128 * g:128 * g + 128] for i in range(OCC)]
            sq = jnp.zeros((8, 128), F32)
            for h in range(2):
                ys = []
                for m in range(8 * h, 8 * h + 8):
                    part = None
                    for i in range(OCC):
                        term = xs[i] * cexp[m, j, i:i + 1, 128 * g:128 * g + 128]
                        part = term if i == 0 else part + term
                    block = part.astype(BF16)
                    for k in range(4):
                        piece = part[8 * k:8 * k + 8]
                        sq = sq + piece * piece
                    ys.append(block)
                for bit in (1, 2, 4):
                    low = ((lane >> 4) & bit) == 0
                    zs = list(ys)
                    for i in range(8):
                        if i & bit:
                            continue
                        a, c = ys[i], ys[i | bit]
                        zs[i] = jnp.where(low, a, pltpu.roll(c, PAD * bit, 1))
                        zs[i | bit] = jnp.where(low, pltpu.roll(a, 128 - PAD * bit, 1), c)
                    ys = zs
                for s in range(8):
                    out[j * CAP + 8 * g + s, :, 128 * h:128 * h + 128] = ys[s]
            squares[j, :, 128 * g:128 * g + 128] = sq

    def compute_h(t, q):
        for c in range(2):
            blocks(2 * q + c)

    gather(h_units, COUNTS_H, compute_h, lambda t: None)

    total = jnp.sum(squares[...], axis=1)
    group = (iota((256, 128), 0) >> 4) == iota((256, 128), 1)
    sumout[...] = lax.dot_general(total, group.astype(F32), (((1,), (0,)), ((), ())),
                                  precision=lax.Precision.HIGHEST, preferred_element_type=F32)
    sumbuf[ax] = sumout[...]
    copies = []
    for k in range(1, NX):
        peer = lax.rem(ax + k, NX)
        copy = pltpu.make_async_remote_copy(
            sumout, sumbuf.at[ax], x_send.at[k], x_recv.at[k],
            device_id=(row, peer), device_id_type=pl.DeviceIdType.MESH)
        copy.start()
        copies.append(copy)
    for k in range(UNITS):
        for buf, sem in ((dg, d_send), (hg, h_send)):
            ref = buf.at[pl.ds(0, 31), pl.ds(64 * k, 64)]
            pltpu.make_async_copy(ref, ref, sem.at[k]).wait()
    for buf, sem in ((eo, o_send), (em, m_send)):
        ref = buf.at[pl.ds(0, 31)]
        pltpu.make_async_copy(ref, ref, sem.at[0]).wait()
    for copy in copies:
        copy.wait_recv()
    total_out[...] = (sumbuf[0] + sumbuf[1]) + (sumbuf[2] + sumbuf[3])
    for copy in copies:
        copy.wait_send()


def per_device(density, vir_coeffs, occ_coeffs, shell_len, mu_shell, nu_shell, owner):
    hbm = pl.BlockSpec(memory_space=pl.ANY)
    vmem = pl.BlockSpec(memory_space=pltpu.VMEM)
    dma = pltpu.SemaphoreType.DMA
    blocks, total = pl.pallas_call(
        kernel,
        out_shape=(pltpu.VMEM((512, 32, 256), BF16), pltpu.VMEM((NROW, 128), F32)),
        in_specs=[hbm] * 7,
        out_specs=(vmem, vmem),
        scratch_shapes=[
            pltpu.VMEM((NROW, 256, 512), BF16),
            pltpu.VMEM((NROW, 256, 512), BF16),
            pltpu.VMEM((NCHIP, 512, 1024), BF16),
            pltpu.VMEM((NROW, 8, 512), BF16),
            pltpu.VMEM((NROW, 8, 128), I32),
            pltpu.VMEM((NROW, 64), I32),
            pltpu.VMEM((4, 256, 128), F32),
            pltpu.VMEM((8 * NROW, 8, 128), F32),
            pltpu.VMEM((128, 256), BF16),
            pltpu.VMEM((256, 256), F32),
            pltpu.VMEM((PAD, NROW, OCC, 256), F32),
            pltpu.VMEM((NROW, 256), F32),
            pltpu.VMEM((NROW, 8, 256), F32),
            pltpu.VMEM((NX, NROW, 128), F32),
            pltpu.VMEM((NROW, 128), F32),
            pltpu.VMEM((64, 128), I32),
            pltpu.VMEM((NROW, 128), I32),
            pltpu.SMEM((64, 128), I32),
            pltpu.SMEM((NROW, 128), I32),
            dma((6,)), dma((NCHIP,)), dma((UNITS, NROW)), dma((UNITS, NROW)), dma((NROW,)), dma((NROW,)),
            dma((UNITS,)), dma((UNITS,)), dma((1,)), dma((1,)), dma((NX,)), dma((NX,)), dma((2,)),
        ],
        compiler_params=pltpu.CompilerParams(
            collective_id=0, has_side_effects=True, vmem_limit_bytes=48 * 1024 * 1024),
    )(density.reshape(256, 512), vir_coeffs, occ_coeffs, shell_len,
      mu_shell.reshape(2, 128), nu_shell.reshape(2, 128), owner.reshape(2, 128))
    pair_scale = jnp.sqrt(total[:, :CAP].reshape(512) / (128 * PAD * PAD) + 1e-06)
    return blocks, pair_scale


def solution(mesh):
    return jax.shard_map(
        per_device,
        mesh=mesh,
        in_specs=(
            P("aux", None, "rows"),
            P("rows", None),
            P(None, "rows"),
            P(),
            P("rows"),
            P("rows"),
            P("rows", None),
        ),
        out_specs=(P("rows", "aux", None), P("rows")),
        check_vma=False,
    )
```
